32 devices in a mesh: clip: 2 (over y), tile: 8 (over z, x), tm: 2 (over core).
Axes of the slice: x: 2, y: 2, z: 4, core: 2. Of those that a mesh axis runs over, the one named last changes fastest.
Arguments:
- frames_in: bfloat16 [16, 32, 128, 256], P(('clip', 'tm'), 'tile'), parts along dimension 0, may hold values from -6 to 6
- grad_out: bfloat16 [16, 32, 128, 256], P(('clip', 'tm'), 'tile'), parts along dimension 0, may hold values from -6 to 6
- gain_first: float32 [256], replicated, may hold values from 0.5 to 1.5
- gain_second: float32 [256], replicated, may hold values from 0.5 to 1.5
- spatial_first: bfloat16 [3, 3, 256, 256], replicated, may hold values from -0.125 to 0.125
- temporal_first: bfloat16 [3, 256, 256], replicated, may hold values from -0.21875 to 0.21875
- spatial_second: bfloat16 [3, 3, 256, 256], replicated, may hold values from -0.125 to 0.125
- temporal_second: bfloat16 [3, 256, 256], replicated, may hold values from -0.21875 to 0.21875
Outputs:
- grad_in: bfloat16 [16, 32, 128, 256], P(('clip', 'tm'), 'tile'), parts along dimension 0
The draws below stay inside these ranges and needn't reach their ends.
There are 2 independent parts, one for each index of `clip`. The reference program is written for one: setup_inputs(seed, part) draws one part's arguments, and reference() takes and returns one part's arrays. A program takes and returns all parts, laid end to end along the dimension named above; an argument that names none is the same for every part. Nothing has to cross between parts.
All inputs are finite; a program needn't handle non-finite values.
Results may differ from the reference program's by a relative error of at most 0.0054.
Values may be sent and summed in bfloat16 or wider, within the bound.
No kernel may reach another device: no remote copies, remote signals or barrier semaphores. Data moves between devices by JAX's collectives and lax.ppermute only.
A program may use at most 64 MiB of HBM per device.

```python
import jax
import jax.numpy as jnp
from jax import lax

C = 256
COLS = 128
FRAMES = 8
NROWS = 32


def level_of(key, dims, split, least, largest):
    factor_of = 1.0
    for axis_at, blocks in split:
        steps = jax.random.uniform(jax.random.fold_in(jax.random.fold_in(key, 6), axis_at), (blocks,), jnp.float32, least / len(split), largest / len(split))
        factor_of = factor_of * jnp.repeat(jnp.exp(steps), dims[axis_at] // blocks).reshape((-1,) + (1,) * (len(dims) - 1 - axis_at))
    return factor_of


def noise(stream_key, dims, spread, most, cuts=(), held_as=jnp.bfloat16):
    values = spread * jax.random.normal(stream_key, dims, jnp.float32)
    if cuts:
        values = values * level_of(stream_key, dims, cuts, -0.22, 0.18)
    return jnp.clip(values, -most, most).astype(held_as)


def setup_inputs(seed: int = 0, part: int = 0) -> dict:
    key_of = jax.random.split(jax.random.key(seed), 9)
    own_keys = jax.random.split(jax.random.fold_in(key_of[8], part), 9)
    frames_in = noise(own_keys[0], (FRAMES, NROWS, COLS, C), 1.0, 6.0, ((0, 2), (1, 8)))
    grad_out = noise(own_keys[1], (FRAMES, NROWS, COLS, C), 1.0, 6.0, ((0, 2), (1, 8)))
    gain_first = jnp.clip(jax.random.uniform(key_of[2], (C,), jnp.float32, 0.5, 1.5), 0.5, 1.5)
    gain_second = jnp.clip(jax.random.uniform(key_of[3], (C,), jnp.float32, 0.5, 1.5), 0.5, 1.5)
    spatial_first = noise(key_of[4], (3, 3, C, C), (9 * C) ** -0.5, 0.125)
    temporal_first = noise(key_of[5], (3, C, C), (3 * C) ** -0.5, 0.21875)
    spatial_second = noise(key_of[6], (3, 3, C, C), (9 * C) ** -0.5, 0.125)
    temporal_second = noise(key_of[7], (3, C, C), (3 * C) ** -0.5, 0.21875)
    return {"frames_in": frames_in, "grad_out": grad_out, "gain_first": gain_first, "gain_second": gain_second, "spatial_first": spatial_first, "temporal_first": temporal_first, "spatial_second": spatial_second, "temporal_second": temporal_second}


EPS = 1e-06

def rms_scale(values):
    return lax.rsqrt(lax.optimization_barrier(jnp.mean(values * values, axis=-1, keepdims=True)) + EPS)

def silu_slope(values):
    logistic = jax.nn.sigmoid(values)
    return logistic * (1.0 + values * (1.0 - logistic))

def norm_back(upstream, values, inv_scale, gain_vec):
    scaled = upstream * gain_vec
    unit_vals = values * inv_scale
    return inv_scale * (scaled - unit_vals * lax.optimization_barrier(jnp.mean(scaled * unit_vals, axis=-1, keepdims=True)))

def spatial_conv(inputs, kernel):
    return lax.conv_general_dilated(inputs.astype(jnp.float32), kernel.astype(jnp.float32), (1, 1), ((1, 1), (1, 1)), dimension_numbers=('NHWC', 'HWIO', 'NHWC'), precision=lax.Precision.HIGHEST)

def flipped(kernel):
    return jnp.transpose(jnp.flip(kernel, (0, 1)), (0, 1, 3, 2))

def time_taps(padded, kernel, frame_count):
    channels = padded.shape[-1]
    running = jnp.zeros((frame_count * padded.shape[1] * padded.shape[2], channels), jnp.float32)
    for k in range(3):
        running = running + jnp.dot(padded[k:k + frame_count].reshape(-1, channels), kernel[k], preferred_element_type=jnp.float32)
    return running.reshape((frame_count,) + padded.shape[1:])

def time_back(upstream, kernel):
    frame_count = upstream.shape[0]
    zero_edge = jnp.zeros((2,) + upstream.shape[1:], upstream.dtype)
    padded = jnp.concatenate([zero_edge, upstream, zero_edge], 0)
    kernel_back = jnp.transpose(kernel[::-1], (0, 2, 1))
    all_taps = time_taps(padded, kernel_back, frame_count + 2)
    own_taps = all_taps[2:]
    head_tap = own_taps[:1] + all_taps[:1] + all_taps[1:2]
    return jnp.concatenate([head_tap, own_taps[1:]], 0)

def reference(frames_in, grad_out, gain_first, gain_second, spatial_first, temporal_first, spatial_second, temporal_second):
    frame_count = frames_in.shape[0]
    values_one = frames_in.astype(jnp.float32)
    scale_one = rms_scale(values_one)
    normed_one = values_one * scale_one * gain_first
    active_one = jax.nn.silu(normed_one).astype(jnp.bfloat16)
    spatial_out = spatial_conv(active_one, spatial_first).astype(jnp.bfloat16)
    history = jnp.concatenate([spatial_out[:1], spatial_out[:1], spatial_out], 0)
    hidden_one = time_taps(history, temporal_first, frame_count)
    scale_two = rms_scale(hidden_one)
    normed_two = hidden_one * scale_two * gain_second
    grad_space_two = time_back(grad_out, temporal_second).astype(jnp.bfloat16)
    grad_act_two = spatial_conv(grad_space_two, flipped(spatial_second))
    grad_hidden = norm_back(grad_act_two * silu_slope(normed_two), hidden_one, scale_two, gain_second).astype(jnp.bfloat16)
    grad_space_one = time_back(grad_hidden, temporal_first).astype(jnp.bfloat16)
    grad_act_one = spatial_conv(grad_space_one, flipped(spatial_first))
    grad_input = norm_back(grad_act_one * silu_slope(normed_one), values_one, scale_one, gain_first)
    return (grad_out.astype(jnp.float32) + grad_input).astype(jnp.bfloat16)
```

```python
import functools

import jax
import jax.numpy as jnp
from jax import lax
from jax.experimental import pallas as pl
from jax.experimental.pallas import tpu as pltpu
from jax.sharding import PartitionSpec as P

EPS = 1e-06
F32 = jnp.float32
BF16 = jnp.bfloat16
VMEM = pl.BlockSpec(memory_space=pltpu.VMEM)
SMEM = pl.BlockSpec(memory_space=pltpu.SMEM)


def shape_of(shape, dtype=BF16):
    return jax.ShapeDtypeStruct(shape, dtype)


def call(kernel, out_shape, flops, *args, scalars=0, aliases=None, name=None):
    outs = jax.tree.leaves(out_shape)
    moved = sum(a.size * a.dtype.itemsize for a in args) + sum(o.size * o.dtype.itemsize for o in outs)
    return pl.pallas_call(
        kernel,
        out_shape=out_shape,
        in_specs=[SMEM] * scalars + [VMEM] * (len(args) - scalars),
        out_specs=jax.tree.map(lambda _: VMEM, out_shape),
        input_output_aliases=aliases or {},
        compiler_params=pltpu.CompilerParams(vmem_limit_bytes=48 * 2**20),
        cost_estimate=pl.CostEstimate(flops=flops, bytes_accessed=moved, transcendentals=0),
        name=name,
    )(*args)


def dot_nn(lhs, rhs):
    return lax.dot_general(lhs, rhs, (((1,), (0,)), ((), ())), preferred_element_type=F32)


def dot_nt(lhs, rhs):
    return lax.dot_general(lhs, rhs, (((1,), (1,)), ((), ())), preferred_element_type=F32)


def flat(block):
    return block.reshape(-1, block.shape[-1])


def mean_last(values):
    return jnp.mean(values, axis=-1, keepdims=True)


def logistic(values):
    return 0.5 + 0.5 * jnp.tanh(0.5 * values)


def unit_of(values):
    inv = lax.rsqrt(mean_last(values * values) + EPS)
    return inv, values * inv


def silu_of(values, gain):
    _, unit = unit_of(values)
    normed = unit * gain
    return (normed * logistic(normed)).astype(BF16)


def back_of(upstream, values, gain):
    inv, unit = unit_of(values)
    normed = unit * gain
    sig = logistic(normed)
    scaled = upstream * (sig * (1.0 + normed * (1.0 - sig))) * gain
    return inv * (scaled - unit * mean_last(scaled * unit))


def mixed(sides, before, centre, after, cols):
    rows = before.shape[0]
    at = lax.broadcasted_iota(jnp.int32, (rows, 1), 0) & (cols - 1)
    down = jnp.where(at == 0, 0.0, pltpu.roll(before, 1, 0))
    up = jnp.where(at == cols - 1, 0.0, pltpu.roll(after, rows - 1, 0))
    return centre + down + up


def spatial(rows, kernel_ref, cols):
    lhs = jnp.concatenate(rows, axis=1)
    width = rows[0].shape[1]
    parts = [dot_nn(lhs, kernel_ref[:, dj].reshape(3 * width, -1)) for dj in range(3)]
    return mixed(None, parts[0], parts[1], parts[2], cols)


def spatial_back(rows, kernel_ref, cols):
    lhs = jnp.concatenate(rows, axis=1)
    parts = [
        dot_nt(lhs, jnp.concatenate([kernel_ref[2 - di, 2 - dj] for di in range(3)], axis=1))
        for dj in range(3)
    ]
    return mixed(None, parts[0], parts[1], parts[2], cols)


def time_back(padded, kernel_ref, head):
    weights = jnp.concatenate([kernel_ref[2], kernel_ref[1], kernel_ref[0]], axis=1)
    out = []
    for f in range(len(padded) - 2):
        part = dot_nt(jnp.concatenate(padded[f : f + 3], axis=1), weights)
        if f == 0:
            extra = jnp.concatenate([kernel_ref[0], kernel_ref[0], kernel_ref[1]], axis=1)
            part += head * dot_nt(jnp.concatenate([padded[0], padded[1], padded[0]], axis=1), extra)
        out.append(part.astype(BF16))
    return out


def act_kernel(x_ref, gain_ref, k_ref, a_ref, s_ref, tail_ref):
    frames, nrows, cols, width = x_ref.shape
    gain = gain_ref[...]
    for r in range(nrows):
        values = flat(x_ref[:, r]).astype(F32)
        a_ref[r] = silu_of(values, gain).reshape(frames, cols, width)
    for r in range(1, nrows - 1):
        rows = [flat(a_ref[r + d]) for d in (-1, 0, 1)]
        out = spatial(rows, k_ref, cols).astype(BF16).reshape(frames, cols, width)
        s_ref[r - 1] = out
        tail_ref[r - 1] = out[frames - 2 :]


def act_rim_kernel(up_ref, down_ref, a_ref, gain_ref, k_ref, s_ref, tail_ref):
    nrows, frames, cols, width = a_ref.shape
    gain = gain_ref[...]
    above = silu_of(flat(up_ref[...]).astype(F32), gain)
    below = silu_of(flat(down_ref[...]).astype(F32), gain)
    last = nrows - 1
    for at, rows in enumerate(
        [[above, flat(a_ref[0]), flat(a_ref[1])], [flat(a_ref[last - 1]), flat(a_ref[last]), below]]
    ):
        out = spatial(rows, k_ref, cols).astype(BF16).reshape(frames, cols, width)
        s_ref[at] = out
        tail_ref[at] = out[frames - 2 :]


def grad_time_kernel(flag_ref, g_ref, later_ref, k_ref, d_ref, top_ref, low_ref):
    frames, nrows, cols, width = g_ref.shape
    head = flag_ref[0].astype(F32)
    padded = [flat(g_ref[f]) for f in range(frames)] + [flat(later_ref[f]) for f in range(2)]
    for f, out in enumerate(time_back(padded, k_ref, head)):
        out = out.reshape(nrows, cols, width)
        d_ref[:, f] = out
        top_ref[f] = out[0]
        low_ref[f] = out[nrows - 1]


def hidden_kernel(which, flag_ref, s_ref, early_ref, d_ref, up_ref, down_ref, gain_ref, kt_ref, ks_ref, o_ref, head_ref):
    nrows, frames, cols, width = d_ref.shape
    gain = gain_ref[...]
    at_start = flag_ref[0] != 0

    def row_of(r):
        if r < 0:
            return flat(up_ref[...])
        if r == nrows:
            return flat(down_ref[...])
        return flat(d_ref[r])

    for at, r in enumerate(which):
        first = s_ref[at, 0]
        early = [jnp.where(at_start, first, early_ref[at, f]) for f in range(2)]
        line = early + [s_ref[at, f] for f in range(frames)]
        lhs = jnp.concatenate(
            [jnp.concatenate(line[k : k + frames], axis=0) for k in range(3)], axis=1
        )
        hidden = dot_nn(lhs, kt_ref[...].reshape(3 * width, width))
        grad = spatial_back([row_of(r + d) for d in (-1, 0, 1)], ks_ref, cols)
        out = back_of(grad, hidden, gain).astype(BF16).reshape(frames, cols, width)
        o_ref[at] = out
        head_ref[at] = out[:2]


def back_time_kernel(flag_ref, dh_ref, later_ref, k_ref, d_ref):
    rows, frames, cols, width = dh_ref.shape
    head = flag_ref[0].astype(F32)
    padded = [flat(dh_ref[:, f]) for f in range(frames)] + [flat(later_ref[:, f]) for f in range(2)]
    for f, out in enumerate(time_back(padded, k_ref, head)):
        d_ref[:, f] = out.reshape(rows, cols, width)


def finish(r, rows, x_ref, g_ref, gain, k_ref, o_ref):
    frames, _, cols, width = x_ref.shape
    grad = spatial_back(rows, k_ref, cols)
    out = back_of(grad, flat(x_ref[:, r]).astype(F32), gain)
    o_ref[:, r] = (flat(g_ref[:, r]).astype(F32) + out).astype(BF16).reshape(frames, cols, width)


def out_kernel(x_ref, g_ref, din_ref, drim_ref, gain_ref, k_ref, o_ref):
    nrows = x_ref.shape[1]
    lines = [flat(drim_ref[0])] + [flat(din_ref[r]) for r in range(nrows - 2)] + [flat(drim_ref[1])]
    for r in range(1, nrows - 1):
        finish(r, lines[r - 1 : r + 2], x_ref, g_ref, gain_ref[...], k_ref, o_ref)


def out_rim_kernel(x_ref, g_ref, din_ref, drim_ref, up_ref, down_ref, gain_ref, k_ref, part_ref, o_ref):
    nrows = x_ref.shape[1]
    o_ref[:, 1 : nrows - 1] = part_ref[:, 1 : nrows - 1]
    gain = gain_ref[...]
    finish(0, [flat(up_ref[...]), flat(drim_ref[0]), flat(din_ref[0])], x_ref, g_ref, gain, k_ref, o_ref)
    finish(
        nrows - 1,
        [flat(din_ref[nrows - 3]), flat(drim_ref[1]), flat(down_ref[...])],
        x_ref, g_ref, gain, k_ref, o_ref,
    )


def on_device(
    frames_in,
    grad_out,
    gain_first,
    gain_second,
    spatial_first,
    temporal_first,
    spatial_second,
    temporal_second,
):
    frames, nrows, cols, width = frames_in.shape
    tiles, spans = lax.axis_size("tile"), lax.axis_size("tm")
    flag = (lax.axis_index("tm") == 0).astype(jnp.int32).reshape(1)
    gain_first = gain_first.reshape(1, width)
    gain_second = gain_second.reshape(1, width)

    def to_next(block):
        return lax.ppermute(block, "tile", [(i, i + 1) for i in range(tiles - 1)])

    def to_previous(block):
        return lax.ppermute(block, "tile", [(i + 1, i) for i in range(tiles - 1)])

    def to_later(block):
        return lax.ppermute(block, "tm", [(i, i + 1) for i in range(spans - 1)])

    def to_earlier(block):
        return lax.ppermute(block, "tm", [(i + 1, i) for i in range(spans - 1)])

    inner, rims = list(range(1, nrows - 1)), [0, nrows - 1]
    per_tap = 2 * frames * cols * width * width
    row = (frames, cols, width)

    x_up = to_next(frames_in[:, nrows - 1])
    x_down = to_previous(frames_in[:, 0])
    g_later = to_earlier(grad_out[:2])

    d2, d2_top, d2_low = call(
        grad_time_kernel,
        (shape_of((nrows,) + row), shape_of(row), shape_of(row)),
        4 * nrows * per_tap,
        flag, grad_out, g_later, temporal_second, scalars=1, name="grad_time",
    )
    d2_up = to_next(d2_low)
    d2_down = to_previous(d2_top)

    a1, s_in, s_in_tail = call(
        act_kernel,
        (shape_of((nrows,) + row), shape_of((nrows - 2,) + row), shape_of((nrows - 2, 2, cols, width))),
        9 * (nrows - 2) * per_tap,
        frames_in, gain_first, spatial_first, name="act",
    )
    s_in_early = to_later(s_in_tail)

    def hidden(which, s, early, name):
        return call(
            functools.partial(hidden_kernel, which),
            (shape_of((len(which),) + row), shape_of((len(which), 2, cols, width))),
            12 * len(which) * per_tap,
            flag, s, early, d2, d2_up if which == rims else d2_top, d2_down if which == rims else d2_low,
            gain_second, temporal_first, spatial_second, scalars=1, name=name,
        )

    def back_time(dh, later, name):
        return call(
            back_time_kernel, shape_of(dh.shape), 4 * dh.shape[0] * per_tap,
            flag, dh, later, temporal_first, scalars=1, name=name,
        )

    dh_in, dh_in_head = hidden(inner, s_in, s_in_early, "hidden")
    dh_in_later = to_earlier(dh_in_head)

    s_rim, s_rim_tail = call(
        act_rim_kernel,
        (shape_of((2,) + row), shape_of((2, 2, cols, width))),
        18 * per_tap,
        x_up, x_down, a1, gain_first, spatial_first, name="act_rim",
    )
    s_rim_early = to_later(s_rim_tail)

    d1_in = back_time(dh_in, dh_in_later, "back_time")

    dh_rim, dh_rim_head = hidden(rims, s_rim, s_rim_early, "hidden_rim")
    dh_rim_later = to_earlier(dh_rim_head)
    d1_rim = back_time(dh_rim, dh_rim_later, "back_time_rim")
    d1_up = to_next(d1_rim[1])
    d1_down = to_previous(d1_rim[0])

    part = call(
        out_kernel, shape_of(frames_in.shape), 9 * (nrows - 2) * per_tap,
        frames_in, grad_out, d1_in, d1_rim, gain_first, spatial_first, name="out",
    )
    return call(
        out_rim_kernel, shape_of(frames_in.shape), 18 * per_tap,
        frames_in, grad_out, d1_in, d1_rim, d1_up, d1_down, gain_first, spatial_first, part,
        aliases={8: 0}, name="out_rim",
    )


def solution(mesh):
    return jax.shard_map(
        on_device,
        mesh=mesh,
        in_specs=(
            P(("clip", "tm"), "tile", None, None),
            P(("clip", "tm"), "tile", None, None),
            P(),
            P(),
            P(),
            P(),
            P(),
            P(),
        ),
        out_specs=P(("clip", "tm"), "tile", None, None),
        check_vma=False,
    )
```

```python
import functools

import jax
import jax.numpy as jnp
from jax import lax
from jax.experimental import pallas as pl
from jax.experimental.pallas import tpu as pltpu
from jax.sharding import PartitionSpec as P

EPS = 1e-06
START, END, ODD, TOP, LOW = range(5)
F32 = jnp.float32
BF16 = jnp.bfloat16
VMEM = pl.BlockSpec(memory_space=pltpu.VMEM)
SMEM = pl.BlockSpec(memory_space=pltpu.SMEM)


def shape_of(shape, dtype=BF16):
    return jax.ShapeDtypeStruct(shape, dtype)


def call(kernel, out_shape, flops, *args, scalars=0, aliases=None, name=None):
    outs = jax.tree.leaves(out_shape)
    moved = sum(a.size * a.dtype.itemsize for a in args) + sum(o.size * o.dtype.itemsize for o in outs)
    return pl.pallas_call(
        kernel,
        out_shape=out_shape,
        in_specs=[SMEM] * scalars + [VMEM] * (len(args) - scalars),
        out_specs=jax.tree.map(lambda _: VMEM, out_shape),
        input_output_aliases=aliases or {},
        compiler_params=pltpu.CompilerParams(vmem_limit_bytes=48 * 2**20),
        cost_estimate=pl.CostEstimate(flops=flops, bytes_accessed=moved, transcendentals=0),
        name=name,
    )(*args)


def dot_nn(lhs, rhs):
    return lax.dot_general(lhs, rhs, (((1,), (0,)), ((), ())), preferred_element_type=F32)


def dot_nt(lhs, rhs):
    return lax.dot_general(lhs, rhs, (((1,), (1,)), ((), ())), preferred_element_type=F32)


def flat(block):
    return block.reshape(-1, block.shape[-1])


def mean_last(values):
    return jnp.mean(values, axis=-1, keepdims=True)


def logistic(values):
    return 0.5 + 0.5 * jnp.tanh(0.5 * values)


def unit_of(values):
    inv = lax.rsqrt(mean_last(values * values) + EPS)
    return inv, values * inv


def silu_of(values, gain):
    _, unit = unit_of(values)
    normed = unit * gain
    return (normed * logistic(normed)).astype(BF16)


def back_of(upstream, values, gain):
    inv, unit = unit_of(values)
    normed = unit * gain
    sig = logistic(normed)
    scaled = upstream * (sig * (1.0 + normed * (1.0 - sig))) * gain
    return inv * (scaled - unit * mean_last(scaled * unit))


def mixed(before, centre, after, cols):
    rows = before.shape[0]
    at = lax.broadcasted_iota(jnp.int32, (rows, 1), 0) & (cols - 1)
    down = jnp.where(at == 0, 0.0, pltpu.roll(before, 1, 0))
    up = jnp.where(at == cols - 1, 0.0, pltpu.roll(after, rows - 1, 0))
    return centre + down + up


def spatial(rows, kernel_ref, cols):
    lhs = jnp.concatenate(rows, axis=1)
    width = rows[0].shape[1]
    parts = [dot_nn(lhs, kernel_ref[:, dj].reshape(3 * width, -1)) for dj in range(3)]
    return mixed(parts[0], parts[1], parts[2], cols)


def spatial_back(rows, kernel_ref, cols):
    lhs = jnp.concatenate(rows, axis=1)
    parts = [
        dot_nt(lhs, jnp.concatenate([kernel_ref[2 - di, 2 - dj] for di in range(3)], axis=1))
        for dj in range(3)
    ]
    return mixed(parts[0], parts[1], parts[2], cols)


def time_back(padded, kernel_ref, head):
    weights = jnp.concatenate([kernel_ref[2], kernel_ref[1], kernel_ref[0]], axis=1)
    out = []
    for f in range(len(padded) - 2):
        part = dot_nt(jnp.concatenate(padded[f : f + 3], axis=1), weights)
        if f == 0:
            extra = jnp.concatenate([kernel_ref[0], kernel_ref[0], kernel_ref[1]], axis=1)
            part += head * dot_nt(jnp.concatenate([padded[0], padded[1], padded[0]], axis=1), extra)
        out.append(part.astype(BF16))
    return out


def act_kernel(x_ref, gain_ref, k_ref, a_ref, s_ref, tail_ref):
    frames, nrows, cols, width = x_ref.shape
    gain = gain_ref[...]
    for r in range(nrows):
        values = flat(x_ref[:, r]).astype(F32)
        a_ref[r] = silu_of(values, gain).reshape(frames, cols, width)
    for r in range(1, nrows - 1):
        rows = [flat(a_ref[r + d]) for d in (-1, 0, 1)]
        out = spatial(rows, k_ref, cols).astype(BF16).reshape(frames, cols, width)
        s_ref[r - 1] = out
        tail_ref[r - 1] = out[frames - 2 :]


def neighbours(flag_ref, own, other):
    odd, top, low = flag_ref[ODD] != 0, flag_ref[TOP] != 0, flag_ref[LOW] != 0
    above = jnp.where(top, jnp.zeros_like(own), jnp.where(odd, own, other))
    below = jnp.where(low, jnp.zeros_like(own), jnp.where(odd, other, own))
    return above, below


def act_rim_kernel(flag_ref, own_ref, other_ref, a_ref, gain_ref, k_ref, s_ref, tail_ref):
    nrows, frames, cols, width = a_ref.shape
    gain = gain_ref[...]
    above, below = neighbours(flag_ref, flat(own_ref[...]), flat(other_ref[...]))
    above = silu_of(above.astype(F32), gain)
    below = silu_of(below.astype(F32), gain)
    last = nrows - 1
    for at, rows in enumerate(
        [[above, flat(a_ref[0]), flat(a_ref[1])], [flat(a_ref[last - 1]), flat(a_ref[last]), below]]
    ):
        out = spatial(rows, k_ref, cols).astype(BF16).reshape(frames, cols, width)
        s_ref[at] = out
        tail_ref[at] = out[frames - 2 :]


def later_of(flag_ref, block):
    return jnp.where(flag_ref[END] != 0, jnp.zeros_like(block), block)


def grad_time_kernel(flag_ref, g_ref, later_ref, k_ref, d_ref, own_ref, other_ref):
    frames, nrows, cols, width = g_ref.shape
    head = flag_ref[START].astype(F32)
    odd = flag_ref[ODD] != 0
    padded = [flat(g_ref[f]) for f in range(frames)]
    padded += [later_of(flag_ref, flat(later_ref[f])) for f in range(2)]
    for f, out in enumerate(time_back(padded, k_ref, head)):
        out = out.reshape(nrows, cols, width)
        d_ref[:, f] = out
        own_ref[f] = jnp.where(odd, out[0], out[nrows - 1])
        other_ref[f] = jnp.where(odd, out[nrows - 1], out[0])


def hidden_kernel(which, flag_ref, s_ref, early_ref, d_ref, *refs):
    *rim_refs, gain_ref, kt_ref, ks_ref, o_ref, head_ref = refs
    nrows, frames, cols, width = d_ref.shape
    gain = gain_ref[...]
    at_start = flag_ref[START] != 0
    rows = {r: flat(d_ref[r]) for r in range(nrows)}
    if rim_refs:
        rows[-1], rows[nrows] = neighbours(flag_ref, *[flat(ref[...]) for ref in rim_refs])

    for at, r in enumerate(which):
        first = s_ref[at, 0]
        early = [jnp.where(at_start, first, early_ref[at, f]) for f in range(2)]
        line = early + [s_ref[at, f] for f in range(frames)]
        lhs = jnp.concatenate(
            [jnp.concatenate(line[k : k + frames], axis=0) for k in range(3)], axis=1
        )
        hidden = dot_nn(lhs, kt_ref[...].reshape(3 * width, width))
        grad = spatial_back([rows[r + d] for d in (-1, 0, 1)], ks_ref, cols)
        out = back_of(grad, hidden, gain).astype(BF16).reshape(frames, cols, width)
        o_ref[at] = out
        head_ref[at] = out[:2]


def back_time_kernel(flag_ref, dh_ref, later_ref, k_ref, d_ref, *send_refs):
    rows, frames, cols, width = dh_ref.shape
    head = flag_ref[START].astype(F32)
    odd = flag_ref[ODD] != 0
    padded = [flat(dh_ref[:, f]) for f in range(frames)]
    padded += [later_of(flag_ref, flat(later_ref[:, f])) for f in range(2)]
    for f, out in enumerate(time_back(padded, k_ref, head)):
        out = out.reshape(rows, cols, width)
        d_ref[:, f] = out
        if send_refs:
            own_ref, other_ref = send_refs
            own_ref[f] = jnp.where(odd, out[0], out[1])
            other_ref[f] = jnp.where(odd, out[1], out[0])


def finish(r, rows, x_ref, g_ref, gain, k_ref, o_ref):
    frames, _, cols, width = x_ref.shape
    grad = spatial_back(rows, k_ref, cols)
    out = back_of(grad, flat(x_ref[:, r]).astype(F32), gain)
    o_ref[:, r] = (flat(g_ref[:, r]).astype(F32) + out).astype(BF16).reshape(frames, cols, width)


def out_kernel(x_ref, g_ref, din_ref, drim_ref, gain_ref, k_ref, o_ref):
    nrows = x_ref.shape[1]
    lines = [flat(drim_ref[0])] + [flat(din_ref[r]) for r in range(nrows - 2)] + [flat(drim_ref[1])]
    for r in range(1, nrows - 1):
        finish(r, lines[r - 1 : r + 2], x_ref, g_ref, gain_ref[...], k_ref, o_ref)


def out_rim_kernel(flag_ref, x_ref, g_ref, din_ref, drim_ref, own_ref, other_ref, gain_ref, k_ref, part_ref, o_ref):
    nrows = x_ref.shape[1]
    o_ref[:, 1 : nrows - 1] = part_ref[:, 1 : nrows - 1]
    gain = gain_ref[...]
    above, below = neighbours(flag_ref, flat(own_ref[...]), flat(other_ref[...]))
    finish(0, [above, flat(drim_ref[0]), flat(din_ref[0])], x_ref, g_ref, gain, k_ref, o_ref)
    finish(
        nrows - 1,
        [flat(din_ref[nrows - 3]), flat(drim_ref[1]), below],
        x_ref, g_ref, gain, k_ref, o_ref,
    )


def after(value, *earlier):
    return lax.optimization_barrier((value,) + earlier)[0]


def on_device(
    frames_in,
    grad_out,
    gain_first,
    gain_second,
    spatial_first,
    temporal_first,
    spatial_second,
    temporal_second,
):
    frames, nrows, cols, width = frames_in.shape
    tiles, spans = lax.axis_size("tile"), lax.axis_size("tm")
    tile, span = lax.axis_index("tile"), lax.axis_index("tm")
    odd = tile % 2
    flag = jnp.stack([span == 0, span == spans - 1, odd == 1, tile == 0, tile == tiles - 1]).astype(jnp.int32)
    gain_first = gain_first.reshape(1, width)
    gain_second = gain_second.reshape(1, width)

    def swap(block, first):
        pairs = [(i, i + 1) for i in range(first, tiles - 1, 2)]
        route = dict(pairs + [(b, a) for a, b in pairs])
        return lax.ppermute(block, "tile", [(i, route.get(i, i)) for i in range(tiles)])

    def exchange(own, other):
        return swap(own, 0), swap(other, 1)

    def to_later(block):
        return lax.ppermute(block, "tm", [(i, (i + 1) % spans) for i in range(spans)])

    def to_earlier(block):
        return lax.ppermute(block, "tm", [((i + 1) % spans, i) for i in range(spans)])

    inner, rims = list(range(1, nrows - 1)), [0, nrows - 1]
    per_tap = 2 * frames * cols * width * width
    row = (frames, cols, width)

    g_later = to_earlier(grad_out[:2])
    x_rims = exchange(
        *[lax.dynamic_index_in_dim(frames_in, at, 1, keepdims=False) for at in ((1 - odd) * (nrows - 1), odd * (nrows - 1))]
    )

    d2, *d2_send = call(
        grad_time_kernel,
        (shape_of((nrows,) + row), shape_of(row), shape_of(row)),
        4 * nrows * per_tap,
        flag, grad_out, g_later, temporal_second, scalars=1, name="grad_time",
    )
    d2_rims = exchange(*d2_send)

    a1, s_in, s_in_tail = call(
        act_kernel,
        (shape_of((nrows,) + row), shape_of((nrows - 2,) + row), shape_of((nrows - 2, 2, cols, width))),
        9 * (nrows - 2) * per_tap,
        frames_in, after(gain_first, d2), spatial_first, name="act",
    )
    s_in_early = to_later(s_in_tail)

    def hidden(which, s, early, extra, gain, name):
        return call(
            functools.partial(hidden_kernel, which),
            (shape_of((len(which),) + row), shape_of((len(which), 2, cols, width))),
            12 * len(which) * per_tap,
            flag, s, early, d2, *extra, gain, temporal_first, spatial_second, scalars=1, name=name,
        )

    def back_time(dh, later, name, sends):
        return call(
            back_time_kernel, (shape_of(dh.shape),) + (shape_of(row),) * sends, 4 * dh.shape[0] * per_tap,
            flag, dh, later, temporal_first, scalars=1, name=name,
        )

    s_rim, s_rim_tail = call(
        act_rim_kernel,
        (shape_of((2,) + row), shape_of((2, 2, cols, width))),
        18 * per_tap,
        flag, *x_rims, a1, gain_first, spatial_first, scalars=1, name="act_rim",
    )
    s_rim_early = to_later(s_rim_tail)

    dh_in, dh_in_head = hidden(inner, s_in, s_in_early, (), after(gain_second, s_rim), "hidden")
    (d1_in,) = back_time(dh_in, to_earlier(dh_in_head), "back_time", 0)

    dh_rim, dh_rim_head = hidden(rims, s_rim, s_rim_early, d2_rims, after(gain_second, dh_in), "hidden_rim")
    d1_rim, *d1_send = back_time(dh_rim, to_earlier(dh_rim_head), "back_time_rim", 2)
    d1_rims = exchange(*d1_send)

    part = call(
        out_kernel, shape_of(frames_in.shape), 9 * (nrows - 2) * per_tap,
        frames_in, grad_out, d1_in, d1_rim, gain_first, spatial_first, name="out",
    )
    return call(
        out_rim_kernel, shape_of(frames_in.shape), 18 * per_tap,
        flag, frames_in, grad_out, d1_in, d1_rim, *d1_rims, gain_first, spatial_first, part,
        scalars=1, aliases={9: 0}, name="out_rim",
    )


def solution(mesh):
    return jax.shard_map(
        on_device,
        mesh=mesh,
        in_specs=(
            P(("clip", "tm"), "tile", None, None),
            P(("clip", "tm"), "tile", None, None),
            P(),
            P(),
            P(),
            P(),
            P(),
            P(),
        ),
        out_specs=P(("clip", "tm"), "tile", None, None),
        check_vma=False,
    )
```

```python
import functools

import jax
import jax.numpy as jnp
from jax import lax
from jax.experimental import pallas as pl
from jax.experimental.pallas import tpu as pltpu
from jax.sharding import PartitionSpec as P

EPS = 1e-06
F32 = jnp.float32
BF16 = jnp.bfloat16
VMEM = pl.BlockSpec(memory_space=pltpu.VMEM)
ANY = pl.BlockSpec(memory_space=pl.ANY)
RIM = 16


def shape_of(*shape):
    return jax.ShapeDtypeStruct(shape, BF16)


def call(kernel, outs, flops, *args, aliases=None, scratch=(), any_in=(), any_out=(), vmem=40, name=None):
    moved = sum(a.size * a.dtype.itemsize for a in (*args, *outs))
    return pl.pallas_call(
        kernel,
        out_shape=tuple(outs),
        in_specs=[ANY if i in any_in else VMEM for i in range(len(args))],
        out_specs=tuple(ANY if i in any_out else VMEM for i in range(len(outs))),
        scratch_shapes=scratch,
        input_output_aliases=aliases or {},
        compiler_params=pltpu.CompilerParams(vmem_limit_bytes=vmem * 2**20),
        cost_estimate=pl.CostEstimate(flops=flops, bytes_accessed=moved, transcendentals=0),
        name=name,
    )(*args)


def dot_nn(lhs, rhs):
    return lax.dot_general(lhs, rhs, (((1,), (0,)), ((), ())), preferred_element_type=F32)


def dot_nt(lhs, rhs):
    return lax.dot_general(lhs, rhs, (((1,), (1,)), ((), ())), preferred_element_type=F32)


def flat(block):
    return block.reshape(-1, block.shape[-1])


def mean_last(values):
    return jnp.mean(values, axis=-1, keepdims=True)


def logistic(values):
    return 0.5 + 0.5 * jnp.tanh(0.5 * values)


def unit_of(values):
    inv = lax.rsqrt(mean_last(values * values) + EPS)
    return inv, values * inv


def silu_of(values, gain):
    _, unit = unit_of(values)
    normed = unit * gain
    return (normed * logistic(normed)).astype(BF16)


def back_of(upstream, values, gain):
    inv, unit = unit_of(values)
    normed = unit * gain
    sig = logistic(normed)
    scaled = upstream * (sig * (1.0 + normed * (1.0 - sig))) * gain
    return inv * (scaled - unit * mean_last(scaled * unit))


def mixed(before, centre, after_it, lo, hi, cols):
    rows, span = before.shape[0], hi - lo
    at = lax.rem(lax.broadcasted_iota(jnp.int32, (rows, 1), 0), span) + lo
    down = pltpu.roll(before, 1, 0)
    up = pltpu.roll(after_it, rows - 1, 0)
    if lo == 0:
        down = jnp.where(at == 0, 0.0, down)
    if hi == cols:
        up = jnp.where(at == cols - 1, 0.0, up)
    return centre + down + up


def spatial(rows, kernel_ref, cols):
    lhs = jnp.concatenate(rows, axis=1)
    width = rows[0].shape[1]
    parts = [dot_nn(lhs, kernel_ref[:, dj].reshape(3 * width, -1)) for dj in range(3)]
    return mixed(*parts, 0, cols, cols)


def spatial_back(rows, kernel_ref, lo, hi, cols):
    lhs = jnp.concatenate(rows, axis=1)
    parts = [
        dot_nt(lhs, jnp.concatenate([kernel_ref[2 - di, 2 - dj] for di in range(3)], axis=1))
        for dj in range(3)
    ]
    return mixed(*parts, lo, hi, cols)


def time_back(padded, kernel_ref):
    head = (lax.axis_index("tm") == 0).astype(F32)
    weights = jnp.concatenate([kernel_ref[2], kernel_ref[1], kernel_ref[0]], axis=1)
    out = []
    for f in range(len(padded) - 2):
        part = dot_nt(jnp.concatenate(padded[f : f + 3], axis=1), weights)
        if f == 0:
            extra = jnp.concatenate([kernel_ref[0], kernel_ref[0], kernel_ref[1]], axis=1)
            part += head * dot_nt(jnp.concatenate([padded[0], padded[1], padded[0]], axis=1), extra)
        out.append(part.astype(BF16))
    return out


def later_of(block):
    last = lax.axis_index("tm") == lax.axis_size("tm") - 1
    return jnp.where(last, jnp.zeros_like(block), block)


def is_odd():
    return lax.rem(lax.axis_index("tile"), 2) == 1


def to_send(top, low):
    odd = is_odd()
    return jnp.where(odd, top, low), jnp.where(odd, low, top)


def neighbours(own, other):
    tile, odd = lax.axis_index("tile"), is_odd()
    above = jnp.where(tile == 0, jnp.zeros_like(own), jnp.where(odd, own, other))
    below = jnp.where(tile == lax.axis_size("tile") - 1, jnp.zeros_like(own), jnp.where(odd, other, own))
    return above, below


def spans_of(bounds):
    return list(zip(bounds[:-1], bounds[1:]))


def window(refs, bounds, lo, hi, pick=lambda ref: ref):
    parts = []
    for ref, (a, b) in zip(refs, spans_of(bounds)):
        if max(a, lo) < min(b, hi):
            parts.append(pick(ref)[:, max(a, lo) - a : min(b, hi) - a])
    return flat(parts[0] if len(parts) == 1 else jnp.concatenate(parts, axis=1))


def run_all(copies):
    for copy in copies:
        copy.start()
    for copy in copies:
        copy.wait()


def rims_kernel(x_ref, own_ref, other_ref, sems):
    nrows = x_ref.shape[1]
    odd = lax.rem(lax.axis_index("tile"), 2)
    run_all(
        [
            pltpu.make_async_copy(x_ref.at[:, (1 - odd) * (nrows - 1)], own_ref, sems.at[0]),
            pltpu.make_async_copy(x_ref.at[:, odd * (nrows - 1)], other_ref, sems.at[1]),
        ]
    )


def head_kernel(g_ref, head_ref, sems):
    run_all([pltpu.make_async_copy(g_ref.at[pl.ds(0, 2)], head_ref, sems.at[0])])


def act_kernel(x_ref, gain_ref, k_ref, a_ref, s_ref, tail_ref):
    frames, nrows, cols, width = x_ref.shape
    gain = gain_ref[...]
    for r in range(nrows):
        values = flat(x_ref[:, r]).astype(F32)
        a_ref[r] = silu_of(values, gain).reshape(frames, cols, width)
    for r in range(1, nrows - 1):
        rows = [flat(a_ref[r + d]) for d in (-1, 0, 1)]
        out = spatial(rows, k_ref, cols).astype(BF16).reshape(frames, cols, width)
        s_ref[r - 1] = out
        tail_ref[r - 1] = out[frames - 2 :]


def act_rim_kernel(own_ref, other_ref, a_ref, gain_ref, k_ref, s_ref, tail_ref):
    nrows, frames, cols, width = a_ref.shape
    gain = gain_ref[...]
    above, below = neighbours(flat(own_ref[...]), flat(other_ref[...]))
    above = silu_of(above.astype(F32), gain)
    below = silu_of(below.astype(F32), gain)
    last = nrows - 1
    for at, rows in enumerate(
        [[above, flat(a_ref[0]), flat(a_ref[1])], [flat(a_ref[last - 1]), flat(a_ref[last]), below]]
    ):
        out = spatial(rows, k_ref, cols).astype(BF16).reshape(frames, cols, width)
        s_ref[at] = out
        tail_ref[at] = out[frames - 2 :]


def grad_time_kernel(bounds, g_ref, later_ref, k_ref, d_ref, *send_refs):
    frames, nrows, cols, width = g_ref.shape
    padded = [flat(g_ref[f]) for f in range(frames)] + [later_of(flat(later_ref[f])) for f in range(2)]
    for f, out in enumerate(time_back(padded, k_ref)):
        out = out.reshape(nrows, cols, width)
        d_ref[:, f] = out
        own, other = to_send(out[0], out[nrows - 1])
        for i, (a, b) in enumerate(spans_of(bounds)):
            send_refs[2 * i][f] = own[a:b]
            send_refs[2 * i + 1][f] = other[a:b]


def hidden_kernel(which, lo, hi, bounds, s_ref, early_ref, d_ref, *refs):
    *rim_refs, gain_ref, kt_ref, ks_ref, o_ref, head_ref = refs
    nrows, frames, cols, width = d_ref.shape
    gain = gain_ref[...]
    at_start = lax.axis_index("tm") == 0
    a, b = max(0, lo - RIM), min(cols, hi + RIM)
    rows = {r: flat(d_ref[r, :, a:b]) for r in range(nrows)}
    if rim_refs:
        rows[-1], rows[nrows] = neighbours(*[window(rim_refs[i::2], bounds, a, b) for i in range(2)])

    for at, r in enumerate(which):
        first = s_ref[at, 0, lo:hi]
        early = [jnp.where(at_start, first, early_ref[at, f, lo:hi]) for f in range(2)]
        line = early + [s_ref[at, f, lo:hi] for f in range(frames)]
        lhs = jnp.concatenate(
            [jnp.concatenate(line[k : k + frames], axis=0) for k in range(3)], axis=1
        )
        hidden = dot_nn(lhs, kt_ref[...].reshape(3 * width, width))
        grad = spatial_back([rows[r + d] for d in (-1, 0, 1)], ks_ref, a, b, cols)
        if (a, b) != (lo, hi):
            grad = flat(grad.reshape(frames, b - a, width)[:, lo - a : hi - a])
        out = back_of(grad, hidden, gain).astype(BF16).reshape(frames, hi - lo, width)
        o_ref[at] = out
        head_ref[at] = out[:2]


def back_time_kernel(dh_ref, later_ref, k_ref, d_ref, *send_refs):
    rows, frames, cols, width = dh_ref.shape
    padded = [flat(dh_ref[:, f]) for f in range(frames)] + [later_of(flat(later_ref[:, f])) for f in range(2)]
    for f, out in enumerate(time_back(padded, k_ref)):
        out = out.reshape(rows, cols, width)
        d_ref[:, f] = out
        if send_refs:
            send_refs[0][f], send_refs[1][f] = to_send(out[0], out[1])


def finish(r, lo, hi, a, b, rows, x_ref, g_ref, gain, k_ref):
    frames, _, cols, width = x_ref.shape
    grad = spatial_back(rows, k_ref, a, b, cols)
    if (a, b) != (lo, hi):
        grad = flat(grad.reshape(frames, b - a, width)[:, lo - a : hi - a])
    out = back_of(grad, flat(x_ref[:, r, lo:hi]).astype(F32), gain)
    return (flat(g_ref[:, r, lo:hi]).astype(F32) + out).astype(BF16).reshape(frames, hi - lo, width)


def out_kernel(bounds, x_ref, g_ref, din_ref, *refs):
    *drim_refs, gain_ref, k_ref, o_ref, held, sems = refs
    frames, nrows, cols, width = x_ref.shape
    lines = [window(drim_refs, bounds, 0, cols, lambda ref, i=i: ref[i]) for i in range(2)]
    lines = lines[:1] + [flat(din_ref[r]) for r in range(nrows - 2)] + lines[1:]
    copies = []
    for r in range(1, nrows - 1):
        held[r - 1] = finish(r, 0, cols, 0, cols, lines[r - 1 : r + 2], x_ref, g_ref, gain_ref[...], k_ref)
        copies.append(pltpu.make_async_copy(held.at[r - 1], o_ref.at[:, r], sems.at[r - 1]))
        copies[-1].start()
    for copy in copies:
        copy.wait()


def out_rim_kernel(lo, hi, bounds, x_ref, g_ref, din_ref, *refs):
    *d_refs, gain_ref, k_ref, _, o_ref, held, sems = refs
    frames, nrows, cols, width = x_ref.shape
    count = len(bounds) - 1
    drim_refs, rim_refs = d_refs[:count], d_refs[count:]
    gain = gain_ref[...]
    a, b = max(0, lo - RIM), min(cols, hi + RIM)
    above, below = neighbours(*[window(rim_refs[i::2], bounds, a, b) for i in range(2)])
    top, low = [window(drim_refs, bounds, a, b, lambda ref, i=i: ref[i]) for i in range(2)]
    near, far = [flat(din_ref[r, :, a:b]) for r in (0, nrows - 3)]
    copies = []
    for at, (r, rows) in enumerate([(0, [above, top, near]), (nrows - 1, [far, low, below])]):
        held[at] = finish(r, lo, hi, a, b, rows, x_ref, g_ref, gain, k_ref)
        copies.append(pltpu.make_async_copy(held.at[at], o_ref.at[:, r, lo:hi], sems.at[at]))
        copies[-1].start()
    for copy in copies:
        copy.wait()


def after(value, *earlier):
    return lax.optimization_barrier((value,) + earlier)[0]


def on_device(
    frames_in,
    grad_out,
    gain_first,
    gain_second,
    spatial_first,
    temporal_first,
    spatial_second,
    temporal_second,
):
    frames, nrows, cols, width = frames_in.shape
    tiles, spans = lax.axis_size("tile"), lax.axis_size("tm")
    gain_first = gain_first.reshape(1, width)
    gain_second = gain_second.reshape(1, width)

    def swap(block, first):
        pairs = [(i, i + 1) for i in range(first, tiles - 1, 2)]
        route = dict(pairs + [(b, a) for a, b in pairs])
        return lax.ppermute(block, "tile", [(i, route.get(i, i)) for i in range(tiles)])

    def exchange(own, other):
        return [swap(own, 0), swap(other, 1)]

    def to_later(block):
        return lax.ppermute(block, "tm", [(i, (i + 1) % spans) for i in range(spans)])

    def to_earlier(block):
        return lax.ppermute(block, "tm", [((i + 1) % spans, i) for i in range(spans)])

    inner, rims = list(range(1, nrows - 1)), [0, nrows - 1]
    per_tap = 2 * frames * cols * width * width
    row = (frames, cols, width)
    d2_bounds = [0, cols]
    dh_bounds = [0, cols]
    out_bounds = [0, cols]

    x_send = call(
        rims_kernel, [shape_of(*row), shape_of(*row)], 1, frames_in,
        any_in=(0,), scratch=[pltpu.SemaphoreType.DMA((2,))], name="rims",
    )
    (g_head,) = call(
        head_kernel, [shape_of(2, nrows, cols, width)], 1, after(grad_out, *x_send),
        any_in=(0,), scratch=[pltpu.SemaphoreType.DMA((1,))], name="head",
    )
    g_later = to_earlier(g_head)
    x_rims = exchange(*x_send)

    d2, *d2_send = call(
        functools.partial(grad_time_kernel, d2_bounds),
        [shape_of(nrows, *row)] + [shape_of(frames, b - a, width) for a, b in spans_of(d2_bounds) for _ in range(2)],
        4 * nrows * per_tap,
        grad_out, g_later, temporal_second, name="grad_time",
    )

    a1, s_in, s_in_tail = call(
        act_kernel,
        [shape_of(nrows, *row), shape_of(nrows - 2, *row), shape_of(nrows - 2, 2, cols, width)],
        9 * (nrows - 2) * per_tap,
        frames_in, after(gain_first, d2), spatial_first, name="act",
    )

    def hidden(which, lo, hi, s, early, extra, gain, name):
        return call(
            functools.partial(hidden_kernel, which, lo, hi, d2_bounds),
            [shape_of(len(which), n, hi - lo, width) for n in (frames, 2)],
            12 * len(which) * per_tap * (hi - lo) // cols,
            s, early, d2, *extra, gain, temporal_first, spatial_second, name=name,
        )

    def back_time(dh, later, name, sends):
        return call(
            back_time_kernel,
            [shape_of(*dh.shape)] + [shape_of(*dh.shape[1:])] * sends,
            4 * dh.shape[0] * per_tap * dh.shape[2] // cols,
            dh, later, temporal_first, name=name,
        )

    s_rim, s_rim_tail = call(
        act_rim_kernel,
        [shape_of(2, *row), shape_of(2, 2, cols, width)],
        18 * per_tap,
        *x_rims, a1, gain_first, spatial_first, name="act_rim",
    )
    s_rim_early = to_later(s_rim_tail)

    dh_in, dh_in_head = hidden(inner, 0, cols, s_in, to_later(s_in_tail), (), after(gain_second, s_rim), "hidden")
    (d1_in,) = back_time(dh_in, to_earlier(dh_in_head), "back_time", 0)

    d2_rims = []
    for i in range(len(d2_bounds) - 1):
        d2_rims += exchange(*[after(block, s_rim) if i else block for block in d2_send[2 * i : 2 * i + 2]])

    d1_rim, d1_rims = [], []
    for i, (lo, hi) in enumerate(spans_of(dh_bounds)):
        dh, head = hidden(rims, lo, hi, s_rim, s_rim_early, d2_rims[: 2 * i + 2], after(gain_second, dh_in), "hidden_rim")
        part, *d1_send = back_time(dh, to_earlier(head), "back_time_rim", 2)
        d1_rim.append(part)
        d1_rims += exchange(*d1_send)

    held = lambda n, w: [pltpu.VMEM((n, frames, w, width), BF16), pltpu.SemaphoreType.DMA((n,))]
    (out,) = call(
        functools.partial(out_kernel, dh_bounds),
        [shape_of(*frames_in.shape)],
        9 * (nrows - 2) * per_tap,
        frames_in, grad_out, d1_in, *d1_rim, gain_first, spatial_first,
        any_out=(0,), scratch=held(nrows - 2, cols), name="out",
    )
    for i, (lo, hi) in enumerate(spans_of(out_bounds)):
        operands = [frames_in, grad_out, d1_in, *d1_rim[: i + 1], *d1_rims[: 2 * i + 2], gain_first, spatial_first, out]
        last = len(operands) - 1
        (out,) = call(
            functools.partial(out_rim_kernel, lo, hi, dh_bounds[: i + 2]),
            [shape_of(*frames_in.shape)],
            18 * per_tap * (hi - lo) // cols,
            *operands,
            any_in=(last,), any_out=(0,), aliases={last: 0}, scratch=held(2, hi - lo), name="out_rim",
        )
    return out


def solution(mesh):
    return jax.shard_map(
        on_device,
        mesh=mesh,
        in_specs=(
            P(("clip", "tm"), "tile", None, None),
            P(("clip", "tm"), "tile", None, None),
            P(),
            P(),
            P(),
            P(),
            P(),
            P(),
        ),
        out_specs=P(("clip", "tm"), "tile", None, None),
        check_vma=False,
    )
```

```python
import functools

import jax
import jax.numpy as jnp
from jax import lax
from jax.experimental import pallas as pl
from jax.experimental.pallas import tpu as pltpu
from jax.sharding import PartitionSpec as P

EPS = 1e-06
F32 = jnp.float32
BF16 = jnp.bfloat16
VMEM = pl.BlockSpec(memory_space=pltpu.VMEM)
ANY = pl.BlockSpec(memory_space=pl.ANY)


def shape_of(*shape, dtype=BF16):
    return jax.ShapeDtypeStruct(shape, dtype)


def call(kernel, outs, flops, *args, aliases=None, scratch=(), any_in=(), any_out=(), vmem=40, name=None):
    moved = sum(a.size * a.dtype.itemsize for a in (*args, *outs))
    return pl.pallas_call(
        kernel,
        out_shape=tuple(outs),
        in_specs=[ANY if i in any_in else VMEM for i in range(len(args))],
        out_specs=tuple(ANY if i in any_out else VMEM for i in range(len(outs))),
        scratch_shapes=scratch,
        input_output_aliases=aliases or {},
        compiler_params=pltpu.CompilerParams(vmem_limit_bytes=vmem * 2**20),
        cost_estimate=pl.CostEstimate(flops=flops, bytes_accessed=moved, transcendentals=0),
        name=name,
    )(*args)


def dot_nn(lhs, rhs):
    return lax.dot_general(lhs, rhs, (((1,), (0,)), ((), ())), preferred_element_type=F32)


def dot_nt(lhs, rhs):
    return lax.dot_general(lhs, rhs, (((1,), (1,)), ((), ())), preferred_element_type=F32)


def flat(block):
    return block.reshape(-1, block.shape[-1])


def mean_last(values):
    return jnp.mean(values, axis=-1, keepdims=True)


def logistic(values):
    return 0.5 + 0.5 * jnp.tanh(0.5 * values)


def unit_of(values):
    inv = lax.rsqrt(mean_last(values * values) + EPS)
    return inv, values * inv


def silu_of(values, gain):
    _, unit = unit_of(values)
    normed = unit * gain
    return (normed * logistic(normed)).astype(BF16)


def slope_of(values, gain):
    inv, unit = unit_of(values)
    normed = unit * gain
    sig = logistic(normed)
    return (sig * (1.0 + normed * (1.0 - sig))) * (gain * inv), unit


def back_of(upstream, slope, unit):
    scaled = upstream * slope
    return scaled - unit * mean_last(scaled * unit)


def mixed(before, centre, after_it, cols):
    rows = before.shape[0]
    at = lax.rem(lax.broadcasted_iota(jnp.int32, (rows, 1), 0), cols)
    down = jnp.where(at == 0, 0.0, pltpu.roll(before, 1, 0))
    up = jnp.where(at == cols - 1, 0.0, pltpu.roll(after_it, rows - 1, 0))
    return centre + down + up


def spatial(rows, kernel_ref, cols):
    lhs = jnp.concatenate(rows, axis=1)
    width = kernel_ref.shape[2]
    parts = [dot_nn(lhs, kernel_ref[:, dj].reshape(3 * width, -1)) for dj in range(3)]
    return mixed(*parts, cols)


def spatial_back(rows, taps, kernel_ref, cols):
    lhs = jnp.concatenate(rows, axis=1) if len(rows) > 1 else rows[0]
    parts = []
    for dj in range(3):
        weights = [kernel_ref[2 - di, 2 - dj] for di in taps]
        parts.append(dot_nt(lhs, jnp.concatenate(weights, axis=1) if len(taps) > 1 else weights[0]))
    return mixed(*parts, cols)


def time_back(padded, kernel_ref):
    head = (lax.axis_index("tm") == 0).astype(F32)
    weights = jnp.concatenate([kernel_ref[2], kernel_ref[1], kernel_ref[0]], axis=1)
    out = []
    for f in range(len(padded) - 2):
        part = dot_nt(jnp.concatenate(padded[f : f + 3], axis=1), weights)
        if f == 0:
            extra = jnp.concatenate([kernel_ref[0], kernel_ref[0], kernel_ref[1]], axis=1)
            part += head * dot_nt(jnp.concatenate([padded[0], padded[1], padded[0]], axis=1), extra)
        out.append(part.astype(BF16))
    return out


def later_of(block):
    last = lax.axis_index("tm") == lax.axis_size("tm") - 1
    return jnp.where(last, jnp.zeros_like(block), block)


def is_odd():
    return lax.rem(lax.axis_index("tile"), 2) == 1


def to_send(top, low):
    odd = is_odd()
    return jnp.where(odd, top, low), jnp.where(odd, low, top)


def neighbours(own, other):
    tile, odd = lax.axis_index("tile"), is_odd()
    above = jnp.where(tile == 0, jnp.zeros_like(own), jnp.where(odd, own, other))
    below = jnp.where(tile == lax.axis_size("tile") - 1, jnp.zeros_like(own), jnp.where(odd, other, own))
    return above, below


def run_all(copies):
    for copy in copies:
        copy.start()
    for copy in copies:
        copy.wait()


def rims_kernel(x_ref, own_ref, other_ref, sems):
    nrows = x_ref.shape[1]
    odd = lax.rem(lax.axis_index("tile"), 2)
    run_all(
        [
            pltpu.make_async_copy(x_ref.at[:, (1 - odd) * (nrows - 1)], own_ref, sems.at[0]),
            pltpu.make_async_copy(x_ref.at[:, odd * (nrows - 1)], other_ref, sems.at[1]),
        ]
    )


def act_kernel(x_ref, gain_ref, k_ref, a_ref, s_ref, tail_ref):
    frames, nrows, cols, width = x_ref.shape
    gain = gain_ref[...]
    for r in range(nrows):
        values = flat(x_ref[:, r]).astype(F32)
        a_ref[r] = silu_of(values, gain).reshape(frames, cols, width)
    for r in range(1, nrows - 1):
        rows = [flat(a_ref[r + d]) for d in (-1, 0, 1)]
        out = spatial(rows, k_ref, cols).astype(BF16).reshape(frames, cols, width)
        s_ref[r - 1] = out
        tail_ref[r - 1] = out[frames - 2 :]


def act_rim_kernel(own_ref, other_ref, a_ref, gain_ref, k_ref, s_ref, *tail_refs):
    nrows, frames, cols, width = a_ref.shape
    gain = gain_ref[...]
    above, below = neighbours(flat(own_ref[...]), flat(other_ref[...]))
    above = silu_of(above.astype(F32), gain)
    below = silu_of(below.astype(F32), gain)
    last = nrows - 1
    for at, rows in enumerate(
        [[above, flat(a_ref[0]), flat(a_ref[1])], [flat(a_ref[last - 1]), flat(a_ref[last]), below]]
    ):
        out = spatial(rows, k_ref, cols).astype(BF16).reshape(frames, cols, width)
        s_ref[at] = out
        tail_refs[at][...] = out[frames - 2 :]


def grad_time_kernel(g_ref, later_ref, k_ref, d_ref, own_ref, other_ref):
    frames, nrows, cols, width = g_ref.shape
    padded = [flat(g_ref[f]) for f in range(frames)] + [later_of(flat(later_ref[f])) for f in range(2)]
    for f, out in enumerate(time_back(padded, k_ref)):
        out = out.reshape(nrows, cols, width)
        d_ref[:, f] = out
        own_ref[f], other_ref[f] = to_send(out[0], out[nrows - 1])


def hidden_of(at, s_ref, early_ref, kt_ref):
    frames, cols, width = s_ref.shape[1:]
    at_start = lax.axis_index("tm") == 0
    line = [jnp.where(at_start, s_ref[at, 0], early_ref[f]) for f in range(2)]
    line += [s_ref[at, f] for f in range(frames)]
    lhs = jnp.concatenate([jnp.concatenate(line[k : k + frames], axis=0) for k in range(3)], axis=1)
    return dot_nn(lhs, kt_ref[...].reshape(3 * width, width))


def hidden_kernel(s_ref, early_ref, d_ref, gain_ref, kt_ref, ks_ref, o_ref, head_ref):
    nrows, frames, cols, width = d_ref.shape
    for r in range(1, nrows - 1):
        slope, unit = slope_of(hidden_of(r - 1, s_ref, early_ref.at[r - 1], kt_ref), gain_ref[...])
        grad = spatial_back([flat(d_ref[r + d]) for d in (-1, 0, 1)], [0, 1, 2], ks_ref, cols)
        out = back_of(grad, slope, unit).astype(BF16).reshape(frames, cols, width)
        o_ref[r - 1] = out
        head_ref[r - 1] = out[:2]


def store(refs, at, arrays):
    for ref, array in zip(refs, arrays):
        ref[at] = array.reshape(ref.shape[1:])


def hidden_own_kernel(s_ref, first_ref, last_ref, d_ref, gain_ref, kt_ref, ks_ref, *o_refs):
    nrows, _, cols, _ = d_ref.shape
    for at, (rows, taps) in enumerate([((0, 1), (1, 2)), ((nrows - 2, nrows - 1), (0, 1))]):
        slope, unit = slope_of(hidden_of(at, s_ref, (first_ref, last_ref)[at], kt_ref), gain_ref[...])
        grad = spatial_back([flat(d_ref[r]) for r in rows], taps, ks_ref, cols)
        store(o_refs, at, (grad, slope, unit))


def edges(own_ref, other_ref, k_ref, part_refs):
    cols = own_ref.shape[1]
    for at, row in enumerate(neighbours(flat(own_ref[...]), flat(other_ref[...]))):
        grad, slope, unit = [flat(ref[at]) for ref in part_refs]
        yield at, back_of(grad + spatial_back([row], [2 * at], k_ref, cols), slope, unit)


def hidden_rim_kernel(own_ref, other_ref, ks_ref, grad_ref, slope_ref, unit_ref, o_ref, head_ref):
    for at, out in edges(own_ref, other_ref, ks_ref, (grad_ref, slope_ref, unit_ref)):
        out = out.astype(BF16).reshape(o_ref.shape[1:])
        o_ref[at] = out
        head_ref[at] = out[:2]


def back_time_kernel(dh_ref, later_ref, k_ref, d_ref, *send_refs):
    rows, frames, cols, width = dh_ref.shape
    padded = [flat(dh_ref[:, f]) for f in range(frames)] + [later_of(flat(later_ref[:, f])) for f in range(2)]
    for f, out in enumerate(time_back(padded, k_ref)):
        out = out.reshape(rows, cols, width)
        d_ref[:, f] = out
        if send_refs:
            send_refs[0][f], send_refs[1][f] = to_send(out[0], out[rows - 1])


def lines_of(din_ref, drim_ref):
    return [flat(drim_ref[0])] + [flat(din_ref[r]) for r in range(din_ref.shape[0])] + [flat(drim_ref[1])]


def put(r, at, out, g_ref, held, o_ref, sems):
    held[at] = (flat(g_ref[:, r]).astype(F32) + out).astype(BF16).reshape(held.shape[1:])
    copy = pltpu.make_async_copy(held.at[at], o_ref.at[:, r], sems.at[at])
    copy.start()
    return copy


def out_kernel(x_ref, g_ref, din_ref, drim_ref, gain_ref, k_ref, o_ref, held, sems):
    _, nrows, cols, _ = x_ref.shape
    lines = lines_of(din_ref, drim_ref)
    copies = []
    for r in range(1, nrows - 1):
        grad = spatial_back(lines[r - 1 : r + 2], [0, 1, 2], k_ref, cols)
        out = back_of(grad, *slope_of(flat(x_ref[:, r]).astype(F32), gain_ref[...]))
        copies.append(put(r, r - 1, out, g_ref, held, o_ref, sems))
    for copy in copies:
        copy.wait()


def out_own_kernel(x_ref, din_ref, drim_ref, gain_ref, k_ref, *o_refs):
    _, nrows, cols, _ = x_ref.shape
    lines = lines_of(din_ref, drim_ref)
    for at, (r, rows, taps) in enumerate([(0, lines[:2], (1, 2)), (nrows - 1, lines[-2:], (0, 1))]):
        slope, unit = slope_of(flat(x_ref[:, r]).astype(F32), gain_ref[...])
        store(o_refs, at, (spatial_back(rows, taps, k_ref, cols), slope, unit))


def out_rim_kernel(own_ref, other_ref, k_ref, grad_ref, slope_ref, unit_ref, g_ref, _, o_ref, held, sems):
    nrows = g_ref.shape[1]
    copies = []
    for at, out in edges(own_ref, other_ref, k_ref, (grad_ref, slope_ref, unit_ref)):
        copies.append(put((0, nrows - 1)[at], at, out, g_ref, held, o_ref, sems))
    for copy in copies:
        copy.wait()


def after(value, *earlier):
    return lax.optimization_barrier((value,) + earlier)[0]


def on_device(
    frames_in,
    grad_out,
    gain_first,
    gain_second,
    spatial_first,
    temporal_first,
    spatial_second,
    temporal_second,
):
    frames, nrows, cols, width = frames_in.shape
    tiles, spans = lax.axis_size("tile"), lax.axis_size("tm")
    gain_first = gain_first.reshape(1, width)
    gain_second = gain_second.reshape(1, width)

    def swap(block, first):
        pairs = [(i, i + 1) for i in range(first, tiles - 1, 2)]
        route = dict(pairs + [(b, a) for a, b in pairs])
        return lax.ppermute(block, "tile", [(i, route.get(i, i)) for i in range(tiles)])

    def exchange(own, other):
        return [swap(own, 0), swap(other, 1)]

    def to_later(block):
        return lax.ppermute(block, "tm", [(i, (i + 1) % spans) for i in range(spans)])

    def to_earlier(block):
        return lax.ppermute(block, "tm", [((i + 1) % spans, i) for i in range(spans)])

    per_tap = 2 * frames * cols * width * width
    row = (frames, cols, width)
    inner = nrows - 2
    parts = [shape_of(2, *row, dtype=F32)] * 3
    two = lambda count: [shape_of(count, *row), shape_of(count, 2, cols, width)]
    held = lambda count: [pltpu.VMEM((count, *row), BF16), pltpu.SemaphoreType.DMA((count,))]

    x_send = call(
        rims_kernel, [shape_of(*row)] * 2, 1, frames_in,
        any_in=(0,), scratch=[pltpu.SemaphoreType.DMA((2,))], name="rims",
    )
    g_later = to_earlier(grad_out[:2])
    grads = after(grad_out, *x_send)
    x_rims = exchange(*x_send)

    d2, *d2_send = call(
        grad_time_kernel, [shape_of(nrows, *row)] + [shape_of(*row)] * 2, 4 * nrows * per_tap,
        grads, g_later, temporal_second, name="grad_time",
    )
    d2_rims = exchange(*d2_send)

    a1, s_in, s_in_tail = call(
        act_kernel, [shape_of(nrows, *row)] + two(inner), 9 * inner * per_tap,
        frames_in, after(gain_first, d2), spatial_first, name="act",
    )
    s_rim, *s_rim_tails = call(
        act_rim_kernel, [shape_of(2, *row)] + [shape_of(2, cols, width)] * 2, 18 * per_tap,
        *x_rims, a1, gain_first, spatial_first, name="act_rim",
    )
    s_rim_early = [to_later(tail) for tail in s_rim_tails]

    dh_in, dh_in_head = call(
        hidden_kernel, two(inner), 12 * inner * per_tap,
        s_in, to_later(s_in_tail), d2, after(gain_second, s_rim), temporal_first, spatial_second, name="hidden",
    )
    dh_in_later = to_earlier(dh_in_head)
    own = call(
        hidden_own_kernel, parts, 18 * per_tap,
        s_rim, *s_rim_early, d2, after(gain_second, dh_in), temporal_first, spatial_second, name="hidden_own",
    )
    dh_rim, dh_rim_head = call(
        hidden_rim_kernel, two(2), 6 * per_tap,
        *d2_rims, spatial_second, *own, name="hidden_rim",
    )

    def back_time(dh, later, sends, name):
        return call(
            back_time_kernel, [shape_of(*dh.shape)] + [shape_of(*row)] * sends, 4 * dh.shape[0] * per_tap,
            dh, later, temporal_first, name=name,
        )

    d1_rim, *d1_send = back_time(dh_rim, to_earlier(dh_rim_head), 2, "back_time_rim")
    d1_rims = exchange(*d1_send)
    (d1_in,) = back_time(dh_in, dh_in_later, 0, "back_time")

    own = call(
        out_own_kernel, parts, 12 * per_tap,
        frames_in, d1_in, d1_rim, gain_first, spatial_first, name="out_own",
    )
    (out,) = call(
        out_kernel, [shape_of(*frames_in.shape)], 9 * inner * per_tap,
        frames_in, grads, d1_in, d1_rim, gain_first, spatial_first,
        any_out=(0,), scratch=held(inner), name="out",
    )
    return call(
        out_rim_kernel, [shape_of(*frames_in.shape)], 6 * per_tap,
        *d1_rims, spatial_first, *own, grads, out,
        any_in=(7,), any_out=(0,), aliases={7: 0}, scratch=held(2), name="out_rim",
    )[0]


def solution(mesh):
    return jax.shard_map(
        on_device,
        mesh=mesh,
        in_specs=(
            P(("clip", "tm"), "tile", None, None),
            P(("clip", "tm"), "tile", None, None),
            P(),
            P(),
            P(),
            P(),
            P(),
            P(),
        ),
        out_specs=P(("clip", "tm"), "tile", None, None),
        check_vma=False,
    )
```

```python
import functools

import jax
import jax.numpy as jnp
from jax import lax
from jax.experimental import pallas as pl
from jax.experimental.pallas import tpu as pltpu
from jax.sharding import PartitionSpec as P

EPS = 1e-06
F32 = jnp.float32
BF16 = jnp.bfloat16
VMEM = pl.BlockSpec(memory_space=pltpu.VMEM)
ANY = pl.BlockSpec(memory_space=pl.ANY)


def shape_of(*shape, dtype=BF16):
    return jax.ShapeDtypeStruct(shape, dtype)


def call(kernel, outs, flops, *args, aliases=None, scratch=(), any_in=(), any_out=(), vmem=40, name=None):
    moved = sum(a.size * a.dtype.itemsize for a in (*args, *outs))
    return pl.pallas_call(
        kernel,
        out_shape=tuple(outs),
        in_specs=[ANY if i in any_in else VMEM for i in range(len(args))],
        out_specs=tuple(ANY if i in any_out else VMEM for i in range(len(outs))),
        scratch_shapes=scratch,
        input_output_aliases=aliases or {},
        compiler_params=pltpu.CompilerParams(vmem_limit_bytes=vmem * 2**20),
        cost_estimate=pl.CostEstimate(flops=flops, bytes_accessed=moved, transcendentals=0),
        name=name,
    )(*args)


def dot_nn(lhs, rhs):
    return lax.dot_general(lhs, rhs, (((1,), (0,)), ((), ())), preferred_element_type=F32)


def dot_nt(lhs, rhs):
    return lax.dot_general(lhs, rhs, (((1,), (1,)), ((), ())), preferred_element_type=F32)


def flat(block):
    return block.reshape(-1, block.shape[-1])


def mean_last(values):
    return jnp.mean(values, axis=-1, keepdims=True)


def logistic(values):
    return 0.5 + 0.5 * jnp.tanh(0.5 * values)


def unit_of(values):
    inv = lax.rsqrt(mean_last(values * values) + EPS)
    return inv, values * inv


def silu_of(values, gain):
    _, unit = unit_of(values)
    normed = unit * gain
    return (normed * logistic(normed)).astype(BF16)


def slope_of(values, gain):
    inv, unit = unit_of(values)
    normed = unit * gain
    sig = logistic(normed)
    return (sig * (1.0 + normed * (1.0 - sig))) * (gain * inv), unit


def back_of(upstream, slope, unit):
    scaled = upstream * slope
    return scaled - unit * mean_last(scaled * unit)


def mixed(before, centre, after_it, cols):
    rows = before.shape[0]
    at = lax.rem(lax.broadcasted_iota(jnp.int32, (rows, 1), 0), cols)
    down = jnp.where(at == 0, 0.0, pltpu.roll(before, 1, 0))
    up = jnp.where(at == cols - 1, 0.0, pltpu.roll(after_it, rows - 1, 0))
    return centre + down + up


def spatial(rows, kernel_ref, cols):
    lhs = jnp.concatenate(rows, axis=1)
    width = kernel_ref.shape[2]
    parts = [dot_nn(lhs, kernel_ref[:, dj].reshape(3 * width, -1)) for dj in range(3)]
    return mixed(*parts, cols)


def spatial_back(rows, taps, kernel_ref, cols):
    lhs = jnp.concatenate(rows, axis=1) if len(rows) > 1 else rows[0]
    parts = []
    for dj in range(3):
        weights = [kernel_ref[2 - di, 2 - dj] for di in taps]
        parts.append(dot_nt(lhs, jnp.concatenate(weights, axis=1) if len(taps) > 1 else weights[0]))
    return mixed(*parts, cols)


def time_back(padded, kernel_ref, starts=True):
    head = (lax.axis_index("tm") == 0).astype(F32)
    weights = jnp.concatenate([kernel_ref[2], kernel_ref[1], kernel_ref[0]], axis=1)
    out = []
    for f in range(len(padded) - 2):
        part = dot_nt(jnp.concatenate(padded[f : f + 3], axis=1), weights)
        if f == 0 and starts:
            extra = jnp.concatenate([kernel_ref[0], kernel_ref[0], kernel_ref[1]], axis=1)
            part += head * dot_nt(jnp.concatenate([padded[0], padded[1], padded[0]], axis=1), extra)
        out.append(part.astype(BF16))
    return out


def later_of(block):
    last = lax.axis_index("tm") == lax.axis_size("tm") - 1
    return jnp.where(last, jnp.zeros_like(block), block)


def is_odd():
    return lax.rem(lax.axis_index("tile"), 2) == 1


def to_send(top, low):
    odd = is_odd()
    return jnp.where(odd, top, low), jnp.where(odd, low, top)


def neighbours(own, other):
    tile, odd = lax.axis_index("tile"), is_odd()
    above = jnp.where(tile == 0, jnp.zeros_like(own), jnp.where(odd, own, other))
    below = jnp.where(tile == lax.axis_size("tile") - 1, jnp.zeros_like(own), jnp.where(odd, other, own))
    return above, below


def run_all(copies):
    for copy in copies:
        copy.start()
    for copy in copies:
        copy.wait()


def rims_kernel(x_ref, own_ref, other_ref, sems):
    nrows = x_ref.shape[1]
    odd = lax.rem(lax.axis_index("tile"), 2)
    run_all(
        [
            pltpu.make_async_copy(x_ref.at[:, (1 - odd) * (nrows - 1)], own_ref, sems.at[0]),
            pltpu.make_async_copy(x_ref.at[:, odd * (nrows - 1)], other_ref, sems.at[1]),
        ]
    )


def act_kernel(x_ref, gain_ref, k_ref, a_ref, s_ref, tail_ref):
    frames, nrows, cols, width = x_ref.shape
    gain = gain_ref[...]
    for r in range(nrows):
        values = flat(x_ref[:, r]).astype(F32)
        a_ref[r] = silu_of(values, gain).reshape(frames, cols, width)
    for r in range(1, nrows - 1):
        rows = [flat(a_ref[r + d]) for d in (-1, 0, 1)]
        out = spatial(rows, k_ref, cols).astype(BF16).reshape(frames, cols, width)
        s_ref[r - 1] = out
        tail_ref[r - 1] = out[frames - 2 :]


def act_rim_kernel(own_ref, other_ref, a_ref, gain_ref, k_ref, s_ref, *tail_refs):
    nrows, frames, cols, width = a_ref.shape
    gain = gain_ref[...]
    above, below = neighbours(flat(own_ref[...]), flat(other_ref[...]))
    above = silu_of(above.astype(F32), gain)
    below = silu_of(below.astype(F32), gain)
    last = nrows - 1
    for at, rows in enumerate(
        [[above, flat(a_ref[0]), flat(a_ref[1])], [flat(a_ref[last - 1]), flat(a_ref[last]), below]]
    ):
        out = spatial(rows, k_ref, cols).astype(BF16).reshape(frames, cols, width)
        s_ref[at] = out
        tail_refs[at][...] = out[frames - 2 :]


def grad_time_kernel(g_ref, later_ref, k_ref, d_ref, own_ref, other_ref):
    frames, nrows, cols, width = g_ref.shape
    padded = [flat(g_ref[f]) for f in range(frames)] + [later_of(flat(later_ref[f])) for f in range(2)]
    for f, out in enumerate(time_back(padded, k_ref)):
        out = out.reshape(nrows, cols, width)
        d_ref[:, f] = out
        own_ref[f], other_ref[f] = to_send(out[0], out[nrows - 1])


def hidden_of(at, s_ref, early_ref, kt_ref):
    frames, cols, width = s_ref.shape[1:]
    at_start = lax.axis_index("tm") == 0
    line = [jnp.where(at_start, s_ref[at, 0], early_ref[f]) for f in range(2)]
    line += [s_ref[at, f] for f in range(frames)]
    lhs = jnp.concatenate([jnp.concatenate(line[k : k + frames], axis=0) for k in range(3)], axis=1)
    return dot_nn(lhs, kt_ref[...].reshape(3 * width, width))


def hidden_kernel(s_ref, early_ref, d_ref, gain_ref, kt_ref, ks_ref, o_ref, head_ref):
    nrows, frames, cols, width = d_ref.shape
    for r in range(1, nrows - 1):
        slope, unit = slope_of(hidden_of(r - 1, s_ref, early_ref.at[r - 1], kt_ref), gain_ref[...])
        grad = spatial_back([flat(d_ref[r + d]) for d in (-1, 0, 1)], [0, 1, 2], ks_ref, cols)
        out = back_of(grad, slope, unit).astype(BF16).reshape(frames, cols, width)
        o_ref[r - 1] = out
        head_ref[r - 1] = out[:2]


def store(refs, at, arrays):
    for ref, array in zip(refs, arrays):
        ref[at] = array.reshape(ref.shape[1:])


def grad_own_kernel(d_ref, ks_ref, o_ref):
    nrows, _, cols, _ = d_ref.shape
    for at, (rows, taps) in enumerate([((0, 1), (1, 2)), ((nrows - 2, nrows - 1), (0, 1))]):
        grad = spatial_back([flat(d_ref[r]) for r in rows], taps, ks_ref, cols)
        store((o_ref,), at, (grad,))


def hidden_own_kernel(s_ref, first_ref, last_ref, gain_ref, kt_ref, *o_refs):
    for at, early_ref in enumerate((first_ref, last_ref)):
        store(o_refs, at, slope_of(hidden_of(at, s_ref, early_ref, kt_ref), gain_ref[...]))


def edges(own_ref, other_ref, k_ref, part_refs, f0, f1):
    cols = own_ref.shape[1]
    for at, row in enumerate(neighbours(flat(own_ref[f0:f1]), flat(other_ref[f0:f1]))):
        grad, slope, unit = [flat(ref[at, f0:f1]) for ref in part_refs]
        yield at, back_of(grad + spatial_back([row], [2 * at], k_ref, cols), slope, unit)


def hidden_rim_kernel(f0, f1, own_ref, other_ref, ks_ref, grad_ref, slope_ref, unit_ref, o_ref):
    for at, out in edges(own_ref, other_ref, ks_ref, (grad_ref, slope_ref, unit_ref), f0, f1):
        o_ref[at] = out.astype(BF16).reshape(o_ref.shape[1:])


def frames_of(*refs):
    return [flat(ref[:, f]) for ref in refs for f in range(ref.shape[1])]


def back_time_kernel(dh_ref, later_ref, k_ref, d_ref):
    rows, _, cols, width = dh_ref.shape
    padded = frames_of(dh_ref) + [later_of(block) for block in frames_of(later_ref)]
    for f, out in enumerate(time_back(padded, k_ref)):
        d_ref[:, f] = out.reshape(rows, cols, width)


def back_first_kernel(dh_ref, next_ref, k_ref, d_ref):
    rows, _, cols, width = dh_ref.shape
    for f, out in enumerate(time_back((frames_of(dh_ref, next_ref))[:4], k_ref)):
        d_ref[:, f] = out.reshape(rows, cols, width)


def back_last_kernel(dh_ref, later_ref, first_ref, k_ref, d_ref, own_ref, other_ref):
    rows, frames, cols, width = d_ref.shape
    padded = frames_of(dh_ref) + [later_of(block) for block in frames_of(later_ref)]
    last = [out.reshape(rows, cols, width) for out in time_back(padded, k_ref, starts=False)]
    for f, out in enumerate([first_ref[:, f] for f in range(2)] + last):
        d_ref[:, f] = out
        own_ref[f], other_ref[f] = to_send(out[0], out[rows - 1])


def lines_of(din_ref, drim_ref):
    return [flat(drim_ref[0])] + [flat(din_ref[r]) for r in range(din_ref.shape[0])] + [flat(drim_ref[1])]


def put(r, at, out, g_ref, held, o_ref, sems):
    held[at] = (flat(g_ref[:, r]).astype(F32) + out).astype(BF16).reshape(held.shape[1:])
    copy = pltpu.make_async_copy(held.at[at], o_ref.at[:, r], sems.at[at])
    copy.start()
    return copy


def out_kernel(x_ref, g_ref, din_ref, drim_ref, gain_ref, k_ref, o_ref, held, sems):
    _, nrows, cols, _ = x_ref.shape
    lines = lines_of(din_ref, drim_ref)
    copies = []
    for r in range(1, nrows - 1):
        grad = spatial_back(lines[r - 1 : r + 2], [0, 1, 2], k_ref, cols)
        out = back_of(grad, *slope_of(flat(x_ref[:, r]).astype(F32), gain_ref[...]))
        copies.append(put(r, r - 1, out, g_ref, held, o_ref, sems))
    for copy in copies:
        copy.wait()


def out_own_kernel(x_ref, din_ref, drim_ref, gain_ref, k_ref, *o_refs):
    _, nrows, cols, _ = x_ref.shape
    lines = lines_of(din_ref, drim_ref)
    for at, (r, rows, taps) in enumerate([(0, lines[:2], (1, 2)), (nrows - 1, lines[-2:], (0, 1))]):
        slope, unit = slope_of(flat(x_ref[:, r]).astype(F32), gain_ref[...])
        store(o_refs, at, (spatial_back(rows, taps, k_ref, cols), slope, unit))


def out_rim_kernel(own_ref, other_ref, k_ref, grad_ref, slope_ref, unit_ref, g_ref, _, o_ref, held, sems):
    nrows = g_ref.shape[1]
    copies = []
    for at, out in edges(own_ref, other_ref, k_ref, (grad_ref, slope_ref, unit_ref), 0, g_ref.shape[0]):
        copies.append(put((0, nrows - 1)[at], at, out, g_ref, held, o_ref, sems))
    for copy in copies:
        copy.wait()


def after(value, *earlier):
    return lax.optimization_barrier((value,) + earlier)[0]


def on_device(
    frames_in,
    grad_out,
    gain_first,
    gain_second,
    spatial_first,
    temporal_first,
    spatial_second,
    temporal_second,
):
    frames, nrows, cols, width = frames_in.shape
    tiles, spans = lax.axis_size("tile"), lax.axis_size("tm")
    gain_first = gain_first.reshape(1, width)
    gain_second = gain_second.reshape(1, width)

    def swap(block, first):
        pairs = [(i, i + 1) for i in range(first, tiles - 1, 2)]
        route = dict(pairs + [(b, a) for a, b in pairs])
        return lax.ppermute(block, "tile", [(i, route.get(i, i)) for i in range(tiles)])

    def exchange(own, other):
        return [swap(own, 0), swap(other, 1)]

    def to_later(block):
        return lax.ppermute(block, "tm", [(i, (i + 1) % spans) for i in range(spans)])

    def to_earlier(block):
        return lax.ppermute(block, "tm", [((i + 1) % spans, i) for i in range(spans)])

    per_tap = 2 * frames * cols * width * width
    row = (frames, cols, width)
    inner = nrows - 2
    parts = [shape_of(2, *row, dtype=F32)] * 3
    two = lambda count: [shape_of(count, *row), shape_of(count, 2, cols, width)]
    held = lambda count: [pltpu.VMEM((count, *row), BF16), pltpu.SemaphoreType.DMA((count,))]

    x_send = call(
        rims_kernel, [shape_of(*row)] * 2, 1, frames_in,
        any_in=(0,), scratch=[pltpu.SemaphoreType.DMA((2,))], name="rims",
    )
    g_later = to_earlier(grad_out[:2])
    grads = after(grad_out, *x_send)
    x_rims = exchange(*x_send)

    d2, *d2_send = call(
        grad_time_kernel, [shape_of(nrows, *row)] + [shape_of(*row)] * 2, 4 * nrows * per_tap,
        grads, g_later, temporal_second, name="grad_time",
    )
    d2_rims = exchange(*d2_send)

    a1, s_in, s_in_tail = call(
        act_kernel, [shape_of(nrows, *row)] + two(inner), 9 * inner * per_tap,
        frames_in, after(gain_first, d2), spatial_first, name="act",
    )
    (grad_own,) = call(
        grad_own_kernel, parts[:1], 12 * per_tap,
        d2, after(spatial_second, s_in), name="grad_own",
    )
    s_rim, *s_rim_tails = call(
        act_rim_kernel, [shape_of(2, *row)] + [shape_of(2, cols, width)] * 2, 18 * per_tap,
        *x_rims, a1, after(gain_first, grad_own), spatial_first, name="act_rim",
    )
    s_rim_early = [to_later(tail) for tail in s_rim_tails]

    dh_in, dh_in_head = call(
        hidden_kernel, two(inner), 12 * inner * per_tap,
        s_in, to_later(s_in_tail), d2, after(gain_second, s_rim), temporal_first, spatial_second, name="hidden",
    )
    dh_in_later = to_earlier(dh_in_head)
    own = call(
        hidden_own_kernel, parts[:2], 6 * per_tap,
        s_rim, *s_rim_early, after(gain_second, dh_in), temporal_first, name="hidden_own",
    )
    dh_rim, gate = [], spatial_second
    for f0, f1 in [(0, 2), (2, frames)]:
        dh_rim += call(
            functools.partial(hidden_rim_kernel, f0, f1), [shape_of(2, f1 - f0, cols, width)], 3 * per_tap,
            *d2_rims, gate, grad_own, *own, name="hidden_rim",
        )
        gate = after(spatial_second, dh_rim[0])

    (first,) = call(
        back_first_kernel, [shape_of(2, 2, cols, width)], 4 * per_tap,
        *dh_rim, temporal_first, name="back_first",
    )
    d1_rim, *d1_send = call(
        back_last_kernel, [shape_of(2, *row)] + [shape_of(*row)] * 2, 4 * per_tap,
        dh_rim[1], to_earlier(dh_rim[0]), first, temporal_first, name="back_last",
    )
    d1_rims = exchange(*d1_send)
    (d1_in,) = call(
        back_time_kernel, [shape_of(*dh_in.shape)], 4 * inner * per_tap,
        dh_in, dh_in_later, temporal_first, name="back_time",
    )

    own = call(
        out_own_kernel, parts, 12 * per_tap,
        frames_in, d1_in, d1_rim, gain_first, spatial_first, name="out_own",
    )
    (out,) = call(
        out_kernel, [shape_of(*frames_in.shape)], 9 * inner * per_tap,
        frames_in, grads, d1_in, d1_rim, gain_first, spatial_first,
        any_out=(0,), scratch=held(inner), name="out",
    )
    return call(
        out_rim_kernel, [shape_of(*frames_in.shape)], 6 * per_tap,
        *d1_rims, spatial_first, *own, grads, out,
        any_in=(7,), any_out=(0,), aliases={7: 0}, scratch=held(2), name="out_rim",
    )[0]


def solution(mesh):
    return jax.shard_map(
        on_device,
        mesh=mesh,
        in_specs=(
            P(("clip", "tm"), "tile", None, None),
            P(("clip", "tm"), "tile", None, None),
            P(),
            P(),
            P(),
            P(),
            P(),
            P(),
        ),
        out_specs=P(("clip", "tm"), "tile", None, None),
        check_vma=False,
    )
```

```python
import functools

import jax
import jax.numpy as jnp
from jax import lax
from jax.experimental import pallas as pl
from jax.experimental.pallas import tpu as pltpu
from jax.sharding import PartitionSpec as P

EPS = 1e-06
PAD = 16
F32 = jnp.float32
BF16 = jnp.bfloat16
VMEM = pl.BlockSpec(memory_space=pltpu.VMEM)
ANY = pl.BlockSpec(memory_space=pl.ANY)


def shape_of(*shape, dtype=BF16):
    return jax.ShapeDtypeStruct(shape, dtype)


def call(kernel, outs, flops, *args, aliases=None, scratch=(), any_in=(), any_out=(), vmem=40, name=None):
    moved = sum(a.size * a.dtype.itemsize for a in (*args, *outs))
    return pl.pallas_call(
        kernel,
        out_shape=tuple(outs),
        in_specs=[ANY if i in any_in else VMEM for i in range(len(args))],
        out_specs=tuple(ANY if i in any_out else VMEM for i in range(len(outs))),
        scratch_shapes=scratch,
        input_output_aliases=aliases or {},
        compiler_params=pltpu.CompilerParams(vmem_limit_bytes=vmem * 2**20),
        cost_estimate=pl.CostEstimate(flops=flops, bytes_accessed=moved if flops else 0, transcendentals=0),
        name=name,
    )(*args)


def dot_nn(lhs, rhs):
    return lax.dot_general(lhs, rhs, (((1,), (0,)), ((), ())), preferred_element_type=F32)


def dot_nt(lhs, rhs):
    return lax.dot_general(lhs, rhs, (((1,), (1,)), ((), ())), preferred_element_type=F32)


def flat(block):
    return block.reshape(-1, block.shape[-1])


def mean_last(values):
    return jnp.mean(values, axis=-1, keepdims=True)


def logistic(values):
    return 0.5 + 0.5 * jnp.tanh(0.5 * values)


def unit_of(values):
    inv = lax.rsqrt(mean_last(values * values) + EPS)
    return inv, values * inv


def silu_of(values, gain):
    _, unit = unit_of(values)
    normed = unit * gain
    return (normed * logistic(normed)).astype(BF16)


def slope_of(values, gain):
    inv, unit = unit_of(values)
    normed = unit * gain
    sig = logistic(normed)
    return (sig * (1.0 + normed * (1.0 - sig))) * (gain * inv), unit


def back_of(upstream, slope, unit):
    scaled = upstream * slope
    return scaled - unit * mean_last(scaled * unit)


def mixed(before, centre, after_it, cols):
    rows = before.shape[0]
    at = lax.rem(lax.broadcasted_iota(jnp.int32, (rows, 1), 0), cols)
    down = jnp.where(at == 0, 0.0, pltpu.roll(before, 1, 0))
    up = jnp.where(at == cols - 1, 0.0, pltpu.roll(after_it, rows - 1, 0))
    return centre + down + up


def spatial(rows, kernel_ref, cols):
    lhs = jnp.concatenate(rows, axis=1)
    width = kernel_ref.shape[2]
    parts = [dot_nn(lhs, kernel_ref[:, dj].reshape(3 * width, -1)) for dj in range(3)]
    return mixed(*parts, cols)


def spatial_back(rows, taps, kernel_ref, cols):
    lhs = jnp.concatenate(rows, axis=1) if len(rows) > 1 else rows[0]
    parts = []
    for dj in range(3):
        weights = [kernel_ref[2 - di, 2 - dj] for di in taps]
        parts.append(dot_nt(lhs, jnp.concatenate(weights, axis=1) if len(taps) > 1 else weights[0]))
    return mixed(*parts, cols)


def one_tap(row, di, kernel_ref, cols):
    rows = row.shape[0]
    wide = row.astype(F32)
    at = lax.rem(lax.broadcasted_iota(jnp.int32, (rows, 1), 0), cols)
    before = jnp.where(at == 0, 0.0, pltpu.roll(wide, 1, 0)).astype(BF16)
    after_it = jnp.where(at == cols - 1, 0.0, pltpu.roll(wide, rows - 1, 0)).astype(BF16)
    weights = jnp.concatenate([kernel_ref[2 - di, 2 - dj] for dj in range(3)], axis=1)
    return dot_nt(jnp.concatenate([before, row, after_it], axis=1), weights)


def one_tap(row, di, kernel_ref, cols):
    rows = row.shape[0]
    wide = row.astype(F32)
    at = lax.rem(lax.broadcasted_iota(jnp.int32, (rows, 1), 0), cols)
    before = jnp.where(at == 0, 0.0, pltpu.roll(wide, 1, 0)).astype(BF16)
    after_it = jnp.where(at == cols - 1, 0.0, pltpu.roll(wide, rows - 1, 0)).astype(BF16)
    weights = jnp.concatenate([kernel_ref[2 - di, 2 - dj] for dj in range(3)], axis=1)
    return dot_nt(jnp.concatenate([before, row, after_it], axis=1), weights)


def time_back(padded, kernel_ref, starts=True):
    head = (lax.axis_index("tm") == 0).astype(F32)
    weights = jnp.concatenate([kernel_ref[2], kernel_ref[1], kernel_ref[0]], axis=1)
    count, rows = len(padded) - 2, padded[0].shape[0]
    lhs = jnp.concatenate([jnp.concatenate(padded[k : k + count], axis=0) for k in range(3)], axis=1)
    every = dot_nt(lhs, weights)
    out = [every[f * rows : (f + 1) * rows] for f in range(count)]
    if starts:
        extra = jnp.concatenate([kernel_ref[0], kernel_ref[0], kernel_ref[1]], axis=1)
        out[0] += head * dot_nt(jnp.concatenate([padded[0], padded[1], padded[0]], axis=1), extra)
    return [part.astype(BF16) for part in out]


def later_of(block):
    last = lax.axis_index("tm") == lax.axis_size("tm") - 1
    return jnp.where(last, jnp.zeros_like(block), block)


def is_odd():
    return lax.rem(lax.axis_index("tile"), 2) == 1


def to_send(top, low):
    odd = is_odd()
    return jnp.where(odd, top, low), jnp.where(odd, low, top)


def neighbours(own, other):
    tile, odd = lax.axis_index("tile"), is_odd()
    above = jnp.where(tile == 0, jnp.zeros_like(own), jnp.where(odd, own, other))
    below = jnp.where(tile == lax.axis_size("tile") - 1, jnp.zeros_like(own), jnp.where(odd, other, own))
    return above, below


def run_all(copies):
    for copy in copies:
        copy.start()
    for copy in copies:
        copy.wait()


def rims_kernel(x_ref, own_ref, other_ref, sems):
    nrows = x_ref.shape[1]
    odd = lax.rem(lax.axis_index("tile"), 2)
    run_all(
        [
            pltpu.make_async_copy(x_ref.at[:, (1 - odd) * (nrows - 1)], own_ref, sems.at[0]),
            pltpu.make_async_copy(x_ref.at[:, odd * (nrows - 1)], other_ref, sems.at[1]),
        ]
    )


def act_kernel(x_ref, gain_ref, k_ref, a_ref, s_ref, tail_ref):
    frames, nrows, cols, width = x_ref.shape
    gain = gain_ref[...]
    for r in range(nrows):
        values = flat(x_ref[:, r]).astype(F32)
        a_ref[r] = silu_of(values, gain).reshape(frames, cols, width)
    for r in range(1, nrows - 1):
        rows = [flat(a_ref[r + d]) for d in (-1, 0, 1)]
        out = spatial(rows, k_ref, cols).astype(BF16).reshape(frames, cols, width)
        s_ref[r - 1] = out
        tail_ref[r - 1] = out[frames - 2 :]


def act_rim_kernel(own_ref, other_ref, a_ref, gain_ref, k_ref, s_ref, *tail_refs):
    nrows, frames, cols, width = a_ref.shape
    gain = gain_ref[...]
    above, below = neighbours(flat(own_ref[...]), flat(other_ref[...]))
    above = silu_of(above.astype(F32), gain)
    below = silu_of(below.astype(F32), gain)
    last = nrows - 1
    for at, rows in enumerate(
        [[above, flat(a_ref[0]), flat(a_ref[1])], [flat(a_ref[last - 1]), flat(a_ref[last]), below]]
    ):
        out = spatial(rows, k_ref, cols).astype(BF16).reshape(frames, cols, width)
        s_ref[at] = out
        tail_refs[at][...] = out[frames - 2 :]


def grad_time_kernel(g_ref, later_ref, k_ref, d_ref, own_ref, other_ref):
    frames, nrows, cols, width = g_ref.shape
    padded = [flat(g_ref[f]) for f in range(frames)] + [later_of(flat(later_ref[f])) for f in range(2)]
    for f, out in enumerate(time_back(padded, k_ref)):
        out = out.reshape(nrows, cols, width)
        d_ref[:, f] = out
        own_ref[f], other_ref[f] = to_send(out[0], out[nrows - 1])


def hidden_of(at, s_ref, early_ref, kt_ref):
    frames, cols, width = s_ref.shape[1:]
    at_start = lax.axis_index("tm") == 0
    line = [jnp.where(at_start, s_ref[at, 0], early_ref[f]) for f in range(2)]
    line += [s_ref[at, f] for f in range(frames)]
    lhs = jnp.concatenate([jnp.concatenate(line[k : k + frames], axis=0) for k in range(3)], axis=1)
    return dot_nn(lhs, kt_ref[...].reshape(3 * width, width))


def hidden_kernel(s_ref, early_ref, d_ref, gain_ref, kt_ref, ks_ref, o_ref, head_ref):
    nrows, frames, cols, width = d_ref.shape
    for r in range(1, nrows - 1):
        slope, unit = slope_of(hidden_of(r - 1, s_ref, early_ref.at[r - 1], kt_ref), gain_ref[...])
        grad = spatial_back([flat(d_ref[r + d]) for d in (-1, 0, 1)], [0, 1, 2], ks_ref, cols)
        out = back_of(grad, slope, unit).astype(BF16).reshape(frames, cols, width)
        o_ref[r - 1] = out
        head_ref[r - 1] = out[:2]


def store(refs, at, arrays):
    for ref, array in zip(refs, arrays):
        ref[at] = array.reshape(ref.shape[1:])


def grad_own_kernel(d_ref, ks_ref, o_ref):
    nrows, _, cols, _ = d_ref.shape
    for at, (rows, taps) in enumerate([((0, 1), (1, 2)), ((nrows - 2, nrows - 1), (0, 1))]):
        grad = spatial_back([flat(d_ref[r]) for r in rows], taps, ks_ref, cols)
        store((o_ref,), at, (grad,))


def hidden_own_kernel(s_ref, first_ref, last_ref, gain_ref, kt_ref, *o_refs):
    for at, early_ref in enumerate((first_ref, last_ref)):
        store(o_refs, at, slope_of(hidden_of(at, s_ref, early_ref, kt_ref), gain_ref[...]))


def edges(own_ref, other_ref, k_ref, part_refs, f0, f1):
    cols = own_ref.shape[1]
    for at, row in enumerate(neighbours(flat(own_ref[f0:f1]), flat(other_ref[f0:f1]))):
        grad, slope, unit = [flat(ref[at, f0:f1]) for ref in part_refs]
        yield at, back_of(grad + one_tap(row, 2 * at, k_ref, cols), slope, unit)


def hidden_rim_kernel(f0, f1, own_ref, other_ref, ks_ref, grad_ref, slope_ref, unit_ref, o_ref):
    for at, out in edges(own_ref, other_ref, ks_ref, (grad_ref, slope_ref, unit_ref), f0, f1):
        o_ref[at] = out.astype(BF16).reshape(o_ref.shape[1:])


def frames_of(*refs):
    return [flat(ref[:, f]) for ref in refs for f in range(ref.shape[1])]


def back_time_kernel(dh_ref, later_ref, k_ref, d_ref):
    rows, _, cols, width = dh_ref.shape
    padded = frames_of(dh_ref) + [later_of(block) for block in frames_of(later_ref)]
    for f, out in enumerate(time_back(padded, k_ref)):
        d_ref[:, f] = out.reshape(rows, cols, width)


def back_first_kernel(dh_ref, next_ref, k_ref, d_ref):
    rows, _, cols, width = dh_ref.shape
    for f, out in enumerate(time_back((frames_of(dh_ref, next_ref))[:4], k_ref)):
        d_ref[:, f] = out.reshape(rows, cols, width)


def back_last_kernel(dh_ref, later_ref, first_ref, k_ref, d_ref, own_ref, other_ref):
    rows, frames, cols, width = d_ref.shape
    padded = frames_of(dh_ref) + [later_of(block) for block in frames_of(later_ref)]
    last = [out.reshape(rows, cols, width) for out in time_back(padded, k_ref, starts=False)]
    for f, out in enumerate([first_ref[:, f] for f in range(2)] + last):
        d_ref[:, f] = out
        own_ref[pl.ds(f * cols, cols)], other_ref[f] = to_send(out[0], out[rows - 1])


def lines_of(din_ref, drim_ref):
    return [flat(drim_ref[0])] + [flat(din_ref[r]) for r in range(din_ref.shape[0])] + [flat(drim_ref[1])]


def put(r, at, out, passed, held, o_ref, sems):
    held[at] = (flat(passed).astype(F32) + out).astype(BF16).reshape(held.shape[1:])
    copy = pltpu.make_async_copy(held.at[at], o_ref.at[:, r], sems.at[at])
    copy.start()
    return copy


def out_kernel(x_ref, g_ref, din_ref, drim_ref, gain_ref, k_ref, o_ref, held, sems):
    _, nrows, cols, _ = x_ref.shape
    lines = lines_of(din_ref, drim_ref)
    copies = []
    for r in range(1, nrows - 1):
        grad = spatial_back(lines[r - 1 : r + 2], [0, 1, 2], k_ref, cols)
        out = back_of(grad, *slope_of(flat(x_ref[:, r]).astype(F32), gain_ref[...]))
        copies.append(put(r, r - 1, out, g_ref[:, r], held, o_ref, sems))
    for copy in copies:
        copy.wait()


def out_own_kernel(x_ref, g_ref, din_ref, drim_ref, gain_ref, k_ref, passed_ref, *o_refs):
    _, nrows, cols, _ = x_ref.shape
    lines = lines_of(din_ref, drim_ref)
    for at, (r, rows, taps) in enumerate([(0, lines[:2], (1, 2)), (nrows - 1, lines[-2:], (0, 1))]):
        slope, unit = slope_of(flat(x_ref[:, r]).astype(F32), gain_ref[...])
        store(o_refs, at, (spatial_back(rows, taps, k_ref, cols), slope, unit))
        passed_ref[at] = g_ref[:, r]


def out_rim_kernel(own, halo_ref, k_ref, passed_ref, grad_ref, slope_ref, unit_ref, _, o_ref, held, sems):
    nrows, cols = o_ref.shape[1:3]
    tile = lax.axis_index("tile")
    odd = lax.rem(tile, 2)
    at = 1 - odd if own else odd
    missing = tile == at * (lax.axis_size("tile") - 1)
    row = halo_ref[: grad_ref.shape[1] * cols] if own else flat(halo_ref[...])
    row = jnp.where(missing, jnp.zeros_like(row), row)
    grad, slope, unit = [flat(ref[at]) for ref in (grad_ref, slope_ref, unit_ref)]
    out = back_of(grad + one_tap(row, 2 * at, k_ref, cols), slope, unit)
    put(at * (nrows - 1), 0, out, passed_ref[at], held, o_ref, sems).wait()


def after(value, *earlier):
    return lax.optimization_barrier((value,) + earlier)[0]


def on_device(
    frames_in,
    grad_out,
    gain_first,
    gain_second,
    spatial_first,
    temporal_first,
    spatial_second,
    temporal_second,
):
    frames, nrows, cols, width = frames_in.shape
    tiles, spans = lax.axis_size("tile"), lax.axis_size("tm")
    gain_first = gain_first.reshape(1, width)
    gain_second = gain_second.reshape(1, width)

    def swap(block, first):
        pairs = [(i, i + 1) for i in range(first, tiles - 1, 2)]
        route = dict(pairs + [(b, a) for a, b in pairs])
        return lax.ppermute(block, "tile", [(i, route.get(i, i)) for i in range(tiles)])

    def exchange(own, other):
        return [swap(own, 0), swap(other, 1)]

    def to_later(block):
        return lax.ppermute(block, "tm", [(i, (i + 1) % spans) for i in range(spans)])

    def to_earlier(block):
        return lax.ppermute(block, "tm", [((i + 1) % spans, i) for i in range(spans)])

    per_tap = 2 * frames * cols * width * width
    row = (frames, cols, width)
    inner = nrows - 2
    parts = [shape_of(2, *row, dtype=F32)] * 3
    two = lambda count: [shape_of(count, *row), shape_of(count, 2, cols, width)]
    held = lambda count: [pltpu.VMEM((count, *row), BF16), pltpu.SemaphoreType.DMA((count,))]

    x_send = call(
        rims_kernel, [shape_of(*row)] * 2, 1, frames_in,
        any_in=(0,), scratch=[pltpu.SemaphoreType.DMA((2,))], name="rims",
    )
    g_later = to_earlier(grad_out[:2])
    grads = after(grad_out, *x_send)
    x_rims = exchange(*x_send)

    d2, *d2_send = call(
        grad_time_kernel, [shape_of(nrows, *row)] + [shape_of(*row)] * 2, 4 * nrows * per_tap,
        grads, g_later, temporal_second, name="grad_time",
    )
    d2_rims = exchange(*d2_send)

    a1, s_in, s_in_tail = call(
        act_kernel, [shape_of(nrows, *row)] + two(inner), 9 * inner * per_tap,
        frames_in, after(gain_first, d2), spatial_first, name="act",
    )
    (grad_own,) = call(
        grad_own_kernel, parts[:1], 12 * per_tap,
        d2, after(spatial_second, s_in), name="grad_own",
    )
    s_rim, *s_rim_tails = call(
        act_rim_kernel, [shape_of(2, *row)] + [shape_of(2, cols, width)] * 2, 18 * per_tap,
        *x_rims, a1, after(gain_first, grad_own), spatial_first, name="act_rim",
    )
    s_rim_early = [to_later(tail) for tail in s_rim_tails]

    dh_in, dh_in_head = call(
        hidden_kernel, two(inner), 12 * inner * per_tap,
        s_in, to_later(s_in_tail), d2, after(gain_second, s_rim), temporal_first, spatial_second, name="hidden",
    )
    dh_in_later = to_earlier(dh_in_head)
    own = call(
        hidden_own_kernel, parts[:2], 6 * per_tap,
        s_rim, *s_rim_early, after(gain_second, dh_in), temporal_first, name="hidden_own",
    )
    dh_rim, gate = [], spatial_second
    for f0, f1 in [(0, 2), (2, frames)]:
        dh_rim += call(
            functools.partial(hidden_rim_kernel, f0, f1), [shape_of(2, f1 - f0, cols, width)], 3 * per_tap,
            *d2_rims, gate, grad_own, *own, name="hidden_rim",
        )
        gate = after(spatial_second, dh_rim[0])

    (first,) = call(
        back_first_kernel, [shape_of(2, 2, cols, width)], 4 * per_tap,
        *dh_rim, temporal_first, name="back_first",
    )
    d1_rim, *d1_send = call(
        back_last_kernel, [shape_of(2, *row), shape_of(frames * cols + PAD, width), shape_of(*row)], 4 * per_tap,
        dh_rim[1], to_earlier(dh_rim[0]), first, temporal_first, name="back_last",
    )
    d1_rims = exchange(*d1_send)
    (d1_in,) = call(
        back_time_kernel, [shape_of(*dh_in.shape)], 4 * inner * per_tap,
        dh_in, dh_in_later, temporal_first, name="back_time",
    )

    own = call(
        out_own_kernel, [shape_of(2, *row)] + parts, 12 * per_tap,
        frames_in, grads, d1_in, d1_rim, gain_first, spatial_first, name="out_own",
    )
    (out,) = call(
        out_kernel, [shape_of(*frames_in.shape)], 9 * inner * per_tap,
        frames_in, grads, d1_in, d1_rim, gain_first, spatial_first,
        any_out=(0,), scratch=held(inner), name="out",
    )
    for own_side, halo in ((False, d1_rims[1]), (True, d1_rims[0])):
        (out,) = call(
            functools.partial(out_rim_kernel, own_side), [shape_of(*frames_in.shape)], 0,
            halo, spatial_first, *own, out,
            any_in=(6,), any_out=(0,), aliases={6: 0}, scratch=held(1), name="out_rim",
        )
    return out


def solution(mesh):
    return jax.shard_map(
        on_device,
        mesh=mesh,
        in_specs=(
            P(("clip", "tm"), "tile", None, None),
            P(("clip", "tm"), "tile", None, None),
            P(),
            P(),
            P(),
            P(),
            P(),
            P(),
        ),
        out_specs=P(("clip", "tm"), "tile", None, None),
        check_vma=False,
    )
```
